256 devices in a mesh: loop: 32 (over z, x_lo, core), tok: 8 (over y, x_hi).
Axes of the slice: x: 4 (x_hi: 2, x_lo: 2; x = x_hi * 2 + x_lo), y: 4, z: 8, core: 2. Of those that a mesh axis runs over, the one named last changes fastest.
Arguments:
- features: bfloat16 [4096, 4096], P('loop', 'tok'), may hold values from -6 to 6
- expert_rows: int32 [2, 768], replicated, may hold values from 0 to 4095, as said below
- route_weight: float32 [2, 768], replicated, may hold values from 0.1 to 1
- gate_proj: bfloat16 [2, 4096, 14336], P(None, 'tok', 'loop'), may hold values from -0.09375 to 0.09375
- up_proj: bfloat16 [2, 4096, 14336], P(None, 'tok', 'loop'), may hold values from -0.09375 to 0.09375
- down_proj: bfloat16 [2, 14336, 4096], P(None, 'loop', 'tok'), may hold values from -0.046875 to 0.046875
- out_grad: bfloat16 [4096, 4096], P('loop', 'tok'), may hold values from -6 to 6
Outputs:
- mixed: bfloat16 [4096, 4096], P('loop', 'tok')
- feature_grad: bfloat16 [4096, 4096], P('loop', 'tok')
- gate_grad: bfloat16 [2, 4096, 14336], P(None, 'tok', 'loop')
- up_grad: bfloat16 [2, 4096, 14336], P(None, 'tok', 'loop')
- down_grad: bfloat16 [2, 14336, 4096], P(None, 'loop', 'tok')
The draws below stay inside these ranges and needn't reach their ends.
Inputs may be any that keep to these rules, and one draw needn't show every extreme that they name: `expert_rows`: each expert's list holds 768 distinct tokens in ascending order, and tokens 0 and 4095 are in every list. Of the 128 tokens t with the same t // 128, at most 48 are in one list, and in every list exactly 48 come from one such index.
All inputs are finite; a program needn't handle non-finite values.
Results may differ from the reference program's by a relative error of at most 0.0049.
Values may be sent and summed in bfloat16 or wider, within the bound.
A program may use at most 128 MiB of HBM per device.

```python
import math
import jax
import jax.numpy as jnp

D = 4096
FF = 14336
EXPERTS = 2
TOK_LOOP = 128
ROWS_E = 768
TOKENS = 4096


def draw_expert_rows(key, part):
    loops = TOKENS // TOK_LOOP
    average = ROWS_E // loops
    half = loops // 2
    lists = []
    for expert in range(EXPERTS):
        base = jax.random.fold_in(key, 101 + expert)
        key_shift, key_order, key_place, key_rank = jax.random.split(base, 4)
        shifts = jax.random.randint(key_shift, (half,), 0, average).at[0].set(average)
        counts = average + jnp.concatenate([shifts, -shifts])
        counts = counts[jax.random.permutation(key_order, loops)]
        empty_at = jnp.argmin(counts)
        target = jax.random.randint(key_place, (), 1, loops - 1)
        counts = jnp.roll(counts, target - empty_at)
        scores = jax.random.randint(key_rank, (loops, TOK_LOOP), 0, 1 << 20) * TOK_LOOP + jnp.arange(TOK_LOOP)[None, :]
        scores = scores.at[0, 0].set(-1).at[loops - 1, TOK_LOOP - 1].set(-1)
        ranks = jnp.argsort(jnp.argsort(scores, axis=1), axis=1)
        chosen = (ranks < counts[:, None]).reshape(-1)
        order_key = jnp.where(chosen, 0, TOKENS) + jnp.arange(TOKENS)
        lists.append(jnp.argsort(order_key)[:ROWS_E].astype(jnp.int32))
    return jnp.stack(lists)


def block_scale(key, extent, cuts, least, top_value):
    factor_of = 1.0
    for dim, parts in cuts:
        steps = jax.random.uniform(jax.random.fold_in(jax.random.fold_in(key, 6), dim), (parts,), jnp.float32, least / len(cuts), top_value / len(cuts))
        factor_of = factor_of * jnp.repeat(jnp.exp(steps), extent[dim] // parts).reshape((-1,) + (1,) * (len(extent) - 1 - dim))
    return factor_of


def centred(key, shape, spread, bound, shards=(), held_as=jnp.bfloat16):
    drawn = spread * jax.random.normal(key, shape, jnp.float32)
    if shards:
        drawn = drawn * block_scale(key, shape, shards, -0.22, 0.18)
    return jnp.clip(drawn, -bound, bound).astype(held_as)


def setup_inputs(seed: int = 0) -> dict:
    keys = jax.random.split(jax.random.key(seed), 8)
    features = centred(keys[0], (TOKENS, D), 1.0, 6.0, ((0, 32), (1, 8)))
    expert_rows = draw_expert_rows(jax.random.fold_in(keys[7], 71), 0)
    route_weight = jnp.clip(jnp.exp(jax.random.uniform(keys[2], (EXPERTS, ROWS_E), jnp.float32, math.log(0.1), math.log(1.0))), 0.1, 1.0)
    gate_proj = centred(keys[3], (EXPERTS, D, FF), D ** -0.5, 0.09375, ((1, 8), (2, 32)))
    up_proj = centred(keys[4], (EXPERTS, D, FF), D ** -0.5, 0.09375, ((1, 8), (2, 32)))
    down_proj = centred(keys[5], (EXPERTS, FF, D), FF ** -0.5, 0.046875, ((1, 32), (2, 8)))
    out_grad = centred(keys[6], (TOKENS, D), 1.0, 6.0, ((0, 32), (1, 8)))
    return {"features": features, "expert_rows": expert_rows, "route_weight": route_weight, "gate_proj": gate_proj, "up_proj": up_proj, "down_proj": down_proj, "out_grad": out_grad}


def reference(features, expert_rows, route_weight, gate_proj, up_proj, down_proj, out_grad):
    token_rows = features[expert_rows].astype(jnp.float32)
    grad_rows = out_grad[expert_rows].astype(jnp.float32)
    flat_rows = expert_rows.reshape(-1)
    gate = jnp.einsum("erd,edf->erf", token_rows, gate_proj.astype(jnp.float32))
    upval = jnp.einsum("erd,edf->erf", token_rows, up_proj.astype(jnp.float32))
    back = jnp.einsum("erd,efd->erf", grad_rows, down_proj.astype(jnp.float32))
    weights = route_weight[:, :, None]
    scaled = (weights * jax.nn.silu(gate) * upval).astype(jnp.bfloat16)
    scaled_wide = scaled.astype(jnp.float32)
    sigma = jax.nn.sigmoid(gate)
    weighted = weights * back
    gate_bar = (weighted * upval * sigma * (1.0 + gate * (1.0 - sigma))).astype(jnp.bfloat16)
    up_bar = (weighted * gate * sigma).astype(jnp.bfloat16)
    gate_bar_wide = gate_bar.astype(jnp.float32)
    up_bar_wide = up_bar.astype(jnp.float32)
    term = jnp.einsum("erf,efd->erd", scaled_wide, down_proj.astype(jnp.float32))
    mixed = jnp.zeros((TOKENS, D), jnp.float32).at[flat_rows].add(term.reshape(-1, D))
    input_term = jnp.einsum("erf,edf->erd", gate_bar_wide, gate_proj.astype(jnp.float32))
    input_term = input_term + jnp.einsum("erf,edf->erd", up_bar_wide, up_proj.astype(jnp.float32))
    feature_grad = jnp.zeros((TOKENS, D), jnp.float32).at[flat_rows].add(input_term.reshape(-1, D))
    gate_grad = jnp.einsum("erd,erf->edf", token_rows, gate_bar_wide).astype(jnp.bfloat16)
    up_grad = jnp.einsum("erd,erf->edf", token_rows, up_bar_wide).astype(jnp.bfloat16)
    down_grad = jnp.einsum("erf,erd->efd", scaled_wide, grad_rows).astype(jnp.bfloat16)
    return (mixed.astype(jnp.bfloat16), feature_grad.astype(jnp.bfloat16), gate_grad, up_grad, down_grad)
```

```python
import jax
import jax.numpy as jnp
from jax import lax
from jax.sharding import PartitionSpec as P

SLOTS = 48


def dot(a, b, ca, cb, dtype=jnp.float32):
    return lax.dot_general(a, b, (((ca,), (cb,)), ((), ())), preferred_element_type=jnp.float32).astype(dtype)


def activation(gate, up, back, weights):
    sigma = jax.nn.sigmoid(gate)
    scaled = weights * (gate * sigma) * up
    weighted = weights * back
    gate_bar = weighted * up * sigma * (1.0 + gate * (1.0 - sigma))
    up_bar = weighted * gate * sigma
    return scaled.astype(jnp.bfloat16), gate_bar.astype(jnp.bfloat16), up_bar.astype(jnp.bfloat16)


def local(features, expert_rows, route_weight, gate_proj, up_proj, down_proj, out_grad):
    loops = lax.axis_size("loop")
    toks = lax.axis_size("tok")
    me = lax.axis_index("loop")
    tok = lax.axis_index("tok")
    experts, rows = expert_rows.shape
    held, width = features.shape
    panel = gate_proj.shape[2]
    share = rows // toks

    owner = expert_rows // held
    holder = jnp.arange(loops)
    starts = jnp.sum((owner[:, None, :] < holder[None, :, None]).astype(jnp.int32), axis=2)
    start_of = jnp.sum(jnp.where(owner[:, :, None] == holder, starts[:, None, :], 0), axis=2)
    slot = jnp.arange(rows)[None, :] - start_of
    place = owner * SLOTS + slot

    own = jnp.arange(held) + me * held
    hits = expert_rows[:, :, None] == own
    present = jnp.any(hits, axis=1)
    before = jnp.arange(held)[:, None] > jnp.arange(held)[None, :]
    rank = jnp.sum(jnp.where(before[None], present[:, None, :], False).astype(jnp.int32), axis=2)
    pick = (present[:, None, :] & (rank[:, None, :] == jnp.arange(SLOTS)[None, :, None])).astype(jnp.bfloat16)
    pick = pick.reshape(experts * SLOTS, held)
    both = jnp.concatenate([features, out_grad], axis=1)
    sent = dot(pick, both, 1, 0, jnp.bfloat16)

    everyone = lax.all_gather(sent, "loop", axis=0, tiled=False)
    everyone = everyone.reshape(loops, experts, SLOTS, 2 * width)
    spread = (place[:, :, None] == jnp.arange(loops * SLOTS)).astype(jnp.bfloat16)
    compact = [
        dot(spread[e], everyone[:, e].reshape(loops * SLOTS, 2 * width), 1, 0, jnp.bfloat16)
        for e in range(experts)
    ]
    token_rows = [c[:, :width] for c in compact]
    grad_rows = [c[:, width:] for c in compact]

    parts = []
    for e in range(experts):
        parts.append(
            jnp.stack(
                [
                    dot(token_rows[e], gate_proj[e], 1, 0),
                    dot(token_rows[e], up_proj[e], 1, 0),
                    dot(grad_rows[e], down_proj[e], 1, 1),
                ]
            )
        )
    hidden = jnp.stack(parts).reshape(experts, 3, toks, share, panel).transpose(2, 0, 1, 3, 4)
    hidden = lax.all_to_all(hidden.astype(jnp.bfloat16), "tok", 0, 0, tiled=True)
    hidden = jnp.sum(hidden.astype(jnp.float32), axis=0)
    weights = lax.dynamic_slice_in_dim(route_weight, tok * share, share, axis=1)[:, :, None]
    acts = activation(hidden[:, 0], hidden[:, 1], hidden[:, 2], weights)
    acts = lax.all_gather(jnp.stack(acts), "tok", axis=0, tiled=False)
    acts = acts.transpose(1, 2, 0, 3, 4).reshape(3, experts, rows, panel)
    scaled, gate_bar, up_bar = acts[0], acts[1], acts[2]

    out_part = jnp.concatenate([dot(scaled[e], down_proj[e], 1, 0) for e in range(experts)], axis=0)
    in_part = jnp.concatenate(
        [dot(gate_bar[e], gate_proj[e], 1, 1) + dot(up_bar[e], up_proj[e], 1, 1) for e in range(experts)],
        axis=0,
    )
    summed = lax.psum_scatter(
        jnp.concatenate([out_part, in_part], axis=1), "loop", scatter_dimension=0, tiled=True
    ).astype(jnp.bfloat16)
    summed = lax.all_gather(summed, "loop", axis=0, tiled=True)
    home = (expert_rows.reshape(-1)[None, :] == own[:, None]).astype(jnp.bfloat16)
    result = dot(home, summed, 1, 0, jnp.bfloat16)
    mixed, feature_grad = result[:, :width], result[:, width:]

    gate_grad = jnp.stack([dot(token_rows[e], gate_bar[e], 0, 0, jnp.bfloat16) for e in range(experts)])
    up_grad = jnp.stack([dot(token_rows[e], up_bar[e], 0, 0, jnp.bfloat16) for e in range(experts)])
    down_grad = jnp.stack([dot(scaled[e], grad_rows[e], 0, 0, jnp.bfloat16) for e in range(experts)])
    return (mixed, feature_grad, gate_grad, up_grad, down_grad)


def solution(mesh):
    placed = (
        P("loop", "tok"),
        P(),
        P(),
        P(None, "tok", "loop"),
        P(None, "tok", "loop"),
        P(None, "loop", "tok"),
        P("loop", "tok"),
    )
    return jax.shard_map(
        local,
        mesh=mesh,
        in_specs=placed,
        out_specs=(
            P("loop", "tok"),
            P("loop", "tok"),
            P(None, "tok", "loop"),
            P(None, "tok", "loop"),
            P(None, "loop", "tok"),
        ),
        check_vma=False,
    )
```

```python
import functools
import jax
import jax.numpy as jnp
from jax import lax
from jax.experimental import pallas as pl
from jax.experimental.pallas import tpu as pltpu

from jax.sharding import PartitionSpec as P

MESH = pl.DeviceIdType.MESH
ANY = pl.BlockSpec(memory_space=pl.ANY)
VM = pl.BlockSpec(memory_space=pltpu.VMEM)


def greet(peers):
    barrier = pltpu.get_barrier_semaphore()
    for peer in peers:
        pl.semaphore_signal(barrier, inc=1, device_id=peer, device_id_type=MESH)
    pl.semaphore_wait(barrier, len(peers))


class Sender:
    def __init__(self, send_sems, recv_sems):
        self.send_sems, self.recv_sems, self.copies = send_sems, recv_sems, []

    def start(self, src, dst, peer):
        k = len(self.copies)
        copy = pltpu.make_async_remote_copy(
            src_ref=src, dst_ref=dst, send_sem=self.send_sems.at[k], recv_sem=self.recv_sems.at[k],
            device_id=peer, device_id_type=MESH)
        copy.start()
        self.copies.append(copy)
        return copy

    def drain(self):
        for copy in self.copies:
            copy.wait_send()


def loop_place():
    me = lax.axis_index("loop")
    core = lax.rem(me, 2)
    side = lax.rem(me // 2, 2)
    layer = me // 4
    return layer, side, core


LAYERS = 8


def loop_index(layer, side, core):
    return lax.rem(layer + LAYERS, LAYERS) * 4 + side * 2 + core


def gather_loop_kernel(src, dst, send_sems, recv_sems, own_sem):
    layer, side, core = loop_place()
    other = 1 - side
    at = lambda d, s, c: loop_index(layer + d, s, c)
    up, down = {"loop": at(1, side, core)}, {"loop": at(-1, side, core)}
    across, twin = {"loop": at(0, other, core)}, {"loop": at(0, side, 1 - core)}
    greet((up, down, across, twin))
    own = at(0, side, core)
    sender = Sender(send_sems, recv_sems)
    waits = []

    keep = pltpu.make_async_copy(src, dst.at[own], own_sem)
    keep.start()
    first = sender.start(src.at[0], dst.at[own, 0], across)
    run = {}
    hops = {("own", 1): 3, ("own", -1): 4, ("mate", 1): 4, ("mate", -1): 3, ("q", 1): 4, ("q", -1): 3}

    def step(kind, way, s, ref=None):
        half = 1 if kind == "q" else 0
        block = at(-way * (s - 1), other if kind == "mate" else side, core)
        ref = dst.at[block, half] if ref is None else ref
        run[kind, way, s] = sender.start(ref, dst.at[block, half], up if way == 1 else down)

    for way in (1, -1):
        step("q", way, 1, src.at[1])
        step("own", way, 1, src.at[0])
    twins = [sender.start(src, dst.at[own], twin)]
    crossed = [sender.start(src.at[1], dst.at[own, 1], across)]
    first.wait_recv()
    for way in (1, -1):
        step("mate", way, 1)
    mate = at(0, other, core)
    twins.append(sender.start(dst.at[mate, 0], dst.at[mate, 0], twin))
    done = 0

    def relay_crossed(block):
        crossed[len(relayed)].wait_recv()
        relayed.append(block)
        twins.append(sender.start(dst.at[block, 1], dst.at[block, 1], twin))

    relayed = []
    order = [(0, 0)]
    for s in range(1, 5):
        for kind in ("q", "own", "mate"):
            for way in (1, -1):
                if s > hops[kind, way]:
                    continue
                run[kind, way, s].wait_recv()
                half = 1 if kind == "q" else 0
                block = at(-way * s, other if kind == "mate" else side, core)
                if s < hops[kind, way]:
                    step(kind, way, s + 1)
                if kind == "q":
                    crossed.append(sender.start(dst.at[block, 1], dst.at[block, 1], across))
                    order.append((way, s))
                twins.append(sender.start(dst.at[block, half], dst.at[block, half], twin))
        while len(relayed) < len(order) - 2:
            way, r = order[len(relayed)]
            relay_crossed(at(-way * r, other, core))
    while len(relayed) < len(order):
        way, r = order[len(relayed)]
        relay_crossed(at(-way * r, other, core))
    for copy in twins:
        copy.wait_recv()
    sender.drain()
    keep.wait()


N_LOOP = 21 + 1 + 8 + 31 + 1


def gather_loop(block, collective_id, space=ANY):
    return pl.pallas_call(
        gather_loop_kernel,
        out_shape=jax.ShapeDtypeStruct((32,) + block.shape, block.dtype),
        in_specs=[VM],
        out_specs=space,
        scratch_shapes=[
            pltpu.SemaphoreType.DMA((N_LOOP,)),
            pltpu.SemaphoreType.DMA((N_LOOP,)),
            pltpu.SemaphoreType.DMA,
        ],
        compiler_params=pltpu.CompilerParams(collective_id=collective_id, has_side_effects=True),
        name=f"gather_loop_{collective_id}",
    )(block)


def reduce_loop_kernel(part, out, total, mail, crossing, landing, send_sems, recv_sems):
    layer, side, core = loop_place()
    other = 1 - side
    up, down = ({"loop": loop_index(layer + d, side, core)} for d in (1, -1))
    across, twin = {"loop": loop_index(layer, other, core)}, {"loop": loop_index(layer, side, 1 - core)}
    greet((up, down, across, twin))
    sender = Sender(send_sems, recv_sems)
    spot = lambda d: lax.rem(layer + d + LAYERS, LAYERS)
    far_first = (4, 3, -3, 2, -2, 1, -1, 0)

    twins = {}
    for d in far_first:
        twins[d] = sender.start(part.at[spot(d), :, 1 - core], total.at[spot(d)], twin)
    crossed = {}

    def settle(d):
        twins[d].wait_recv()
        total[spot(d)] = total[spot(d)] + part[spot(d), :, core]
        crossed[d] = sender.start(total.at[spot(d), other, 1], crossing.at[far_first.index(d)], across)

    hops = {("own", 1): 4, ("own", -1): 3, ("mate", 1): 3, ("mate", -1): 4, ("q", 1): 4, ("q", -1): 3}
    run, ready = {}, set()
    kinds = ("own", "mate", "q")

    def mine(kind, d):
        who = other if kind == "mate" else side
        return total.at[spot(d), who, 1 if kind == "q" else 0]

    def box(kind, way, j):
        return mail.at[kinds.index(kind), (0 if way == 1 else 1), j - 1]

    def send(kind, way, j):
        if j > hops[kind, way]:
            return
        d = way * j if j < 4 else 4
        if kind == "q" and d not in ready:
            ready.add(d)
            crossed[d].wait_recv()
            total[spot(d), side, 1] = total[spot(d), side, 1] + crossing[far_first.index(d)]
        src = mine(kind, d)
        if j < hops[kind, way]:
            run[kind, way, j + 1].wait_recv()
            held = box(kind, way, j + 1)
            held[...] = held[...] + src[...]
            src = held
        run[kind, way, j] = sender.start(src, box(kind, way, j), up if way == 1 else down)

    settle(4)
    for j in (4, 3, 2, 1):
        for way in (1, -1):
            send("own", way, j)
            send("mate", way, j)
            if j < 4:
                send("q", way, j + 1)
        if j > 1:
            settle(j - 1)
            settle(1 - j)
        else:
            settle(0)
    for way in (1, -1):
        send("q", way, 1)

    def arrived(kind):
        for way in (1, -1):
            run[kind, way, 1].wait_recv()
        return mine(kind, 0)[...] + box(kind, 1, 1)[...] + box(kind, -1, 1)[...]

    landing[0] = arrived("mate")
    last = sender.start(landing.at[0], landing.at[1], across)
    crossed[0].wait_recv()
    total[spot(0), side, 1] = total[spot(0), side, 1] + crossing[far_first.index(0)]
    own = arrived("own")
    out[1] = arrived("q")
    last.wait_recv()
    out[0] = own + landing[1]
    sender.drain()


N_SUM = 8 + 8 + 21 + 1


def reduce_loop(part, collective_id):
    layers, sides, cores, halves, rows, width = part.shape
    piece = (halves, rows, width)
    return pl.pallas_call(
        reduce_loop_kernel,
        out_shape=jax.ShapeDtypeStruct(piece, part.dtype),
        in_specs=[VM],
        out_specs=VM,
        scratch_shapes=[
            pltpu.VMEM((layers, sides) + piece, part.dtype),
            pltpu.VMEM((3, 2, 4, rows, width), part.dtype),
            pltpu.VMEM((layers, rows, width), part.dtype),
            pltpu.VMEM((2, rows, width), part.dtype),
            pltpu.SemaphoreType.DMA((N_SUM,)),
            pltpu.SemaphoreType.DMA((N_SUM,)),
        ],
        compiler_params=pltpu.CompilerParams(collective_id=collective_id, has_side_effects=True, vmem_limit_bytes=48 << 20),
        name=f"reduce_loop_{collective_id}",
    )(part)


def tok_place():
    layer, side, core = loop_place()
    tok = lax.axis_index("tok")
    tall, high = tok // 2, lax.rem(tok, 2)
    step = lambda d: lax.rem(tall + d + 4, 4) * 2 + high
    peers = {
        "up": {"tok": step(1)},
        "down": {"tok": step(-1)},
        "low": {"loop": loop_index(layer, 1 - side, core)},
        "cross": {"loop": loop_index(layer, 1 - side, core), "tok": tall * 2 + 1 - high},
    }
    return tall, high, peers


def gather_tok_body(src, dst, transit, sender, tall, high, peers, keep=None):
    half_rows = src.shape[1] // 2
    A, B = pl.ds(0, half_rows), pl.ds(half_rows, half_rows)
    at = lambda d, h: lax.rem(tall + d + 4, 4) * 2 + h
    other = 1 - high
    own, mate = at(0, high), at(0, other)
    sent = {}

    def hop(ref, n):
        sent["low", n] = sender.start(ref.at[A], transit.at[n, 0], peers["low"])
        sent["cross", n] = sender.start(ref.at[B], transit.at[n, 1], peers["cross"])

    def pass_on(n, d, half):
        sent["low", n].wait_recv()
        sent["to", n, 0] = sender.start(transit.at[n, 0], dst.at[at(d, high), half, A], peers["cross"])
        sent["cross", n].wait_recv()
        sent["to", n, 1] = sender.start(transit.at[n, 1], dst.at[at(d, other), half, B], peers["low"])

    def landed(n):
        sent["to", n, 0].wait_recv()
        sent["to", n, 1].wait_recv()

    def ring(kind, ref, h, half):
        sent[kind, 1] = sender.start(ref, dst.at[at(0, h), half], peers["up"])
        sent[kind, -1] = sender.start(ref, dst.at[at(0, h), half], peers["down"])

    def onward(kind, h, half):
        for way, piece, to in ((1, A, "up"), (-1, B, "down")):
            sent[kind, way].wait_recv()
            ref = dst.at[at(-way, h), half, piece]
            sent[kind, way, 2] = sender.start(ref, ref, peers[to])

    def closed(kind):
        sent[kind, 1, 2].wait_recv()
        sent[kind, -1, 2].wait_recv()

    hop(src.at[0], 0)
    ring("q", src.at[1], high, 1)
    ring("p", src.at[0], high, 0)
    hop(src.at[1], 1)
    pass_on(0, 0, 0)
    onward("q", high, 1)
    hop(dst.at[at(-1, high), 1], 2)
    hop(dst.at[at(1, high), 1], 3)
    landed(0)
    ring("m", dst.at[mate, 0], other, 0)
    pass_on(1, 0, 1)
    onward("p", high, 0)
    closed("q")
    hop(dst.at[at(2, high), 1], 4)
    pass_on(2, -1, 1)
    pass_on(3, 1, 1)
    onward("m", other, 0)
    pass_on(4, 2, 1)
    closed("p")
    closed("m")
    for n in range(1, 5):
        landed(n)


N_GT = 5 * 4 + 3 * 4


def gather_tok_kernel(src, dst, transit, send_sems, recv_sems, own_sem):
    tall, high, peers = tok_place()
    greet(tuple(peers.values()))
    keep = pltpu.make_async_copy(src, dst.at[tall * 2 + high], own_sem)
    keep.start()
    sender = Sender(send_sems, recv_sems)
    gather_tok_body(src, dst, transit, sender, tall, high, peers)
    sender.drain()
    keep.wait()


def gather_tok(block, collective_id, space=ANY):
    halves, rows, width = block.shape
    return pl.pallas_call(
        gather_tok_kernel,
        out_shape=jax.ShapeDtypeStruct((8,) + block.shape, block.dtype),
        in_specs=[VM],
        out_specs=space,
        scratch_shapes=[
            pltpu.VMEM((5, 2, rows // 2, width), block.dtype),
            pltpu.SemaphoreType.DMA((N_GT,)),
            pltpu.SemaphoreType.DMA((N_GT,)),
            pltpu.SemaphoreType.DMA,
        ],
        compiler_params=pltpu.CompilerParams(collective_id=collective_id, has_side_effects=True),
        name=f"gather_tok_{collective_id}",
    )(block)


N_RT = 5 * 4 + 3 * 4


def reduce_tok_kernel(part, out, post, mail, transit, landing, carry, send_sems, recv_sems):
    tall, high, peers = tok_place()
    greet(tuple(peers.values()))
    sender = Sender(send_sems, recv_sems)
    rows = part.shape[2]
    half_rows = rows // 2
    A, B = pl.ds(0, half_rows), pl.ds(half_rows, half_rows)
    at = lambda d, h: lax.rem(tall + d + 4, 4) * 2 + h
    other = 1 - high
    sent = {}
    f32, bf16 = jnp.float32, jnp.bfloat16

    def hop(n):
        sent["low", n] = sender.start(post.at[n, A], transit.at[n, 0], peers["low"])
        sent["cross", n] = sender.start(post.at[n, B], transit.at[n, 1], peers["cross"])

    def pass_on(n):
        sent["low", n].wait_recv()
        sent["to", n, 0] = sender.start(transit.at[n, 0], landing.at[n, A], peers["cross"])
        sent["cross", n].wait_recv()
        sent["to", n, 1] = sender.start(transit.at[n, 1], landing.at[n, B], peers["low"])

    def landed(n):
        sent["to", n, 0].wait_recv()
        sent["to", n, 1].wait_recv()

    def term(kind, d, rows_of):
        if kind == 2:
            return carry[DS.index(d), rows_of]
        return part[at(d, high if kind == 0 else other), 0, rows_of]

    def far(kind):
        for w, way, piece, to in ((0, 1, A, "up"), (1, -1, B, "down")):
            mail[kind, w, 0, piece] = term(kind, 2, piece).astype(bf16)
            sent[kind, way, 2] = sender.start(mail.at[kind, w, 0, piece], mail.at[kind, w, 1, piece], peers[to])

    def near(kind):
        for w, way, piece, rest, to in ((0, 1, A, B, "up"), (1, -1, B, A, "down")):
            mail[kind, w, 2, rest] = term(kind, way, rest).astype(bf16)
            sent[kind, way, 2].wait_recv()
            mail[kind, w, 2, piece] = (term(kind, way, piece) + mail[kind, w, 1, piece].astype(f32)).astype(bf16)
            sent[kind, way, 1] = sender.start(mail.at[kind, w, 2], mail.at[kind, w, 3], peers[to])

    def whole(kind):
        sent[kind, 1, 1].wait_recv()
        sent[kind, -1, 1].wait_recv()
        everything = pl.ds(0, rows)
        return term(kind, 0, everything) + mail[kind, 0, 3].astype(f32) + mail[kind, 1, 3].astype(f32)

    DS = (2, 1, -1, 0)
    far(1)
    for n, d in enumerate(DS[:3]):
        post[n] = part[at(d, other), 1].astype(bf16)
        hop(n)
    far(0)
    post[3] = part[at(0, other), 1].astype(bf16)
    hop(3)
    near(1)
    pass_on(0)
    near(0)
    pass_on(1)
    pass_on(2)

    def mix(n):
        landed(n)
        carry[n] = part[at(DS[n], high), 1] + landing[n].astype(f32)

    mix(0)
    far(2)
    pass_on(3)
    post[4] = whole(1).astype(bf16)
    hop(4)
    mix(1)
    mix(2)
    near(2)
    pass_on(4)
    mix(3)
    out[1] = whole(2)
    own = whole(0)
    landed(4)
    out[0] = own + landing[4].astype(f32)
    sender.drain()


def reduce_tok(part, collective_id):
    toks, halves, rows, width = part.shape
    bf16 = jnp.bfloat16
    return pl.pallas_call(
        reduce_tok_kernel,
        out_shape=jax.ShapeDtypeStruct((halves, rows, width), part.dtype),
        in_specs=[VM],
        out_specs=VM,
        scratch_shapes=[
            pltpu.VMEM((5, rows, width), bf16),
            pltpu.VMEM((3, 2, 4, rows, width), bf16),
            pltpu.VMEM((5, 2, rows // 2, width), bf16),
            pltpu.VMEM((5, rows, width), bf16),
            pltpu.VMEM((4, rows, width), jnp.float32),
            pltpu.SemaphoreType.DMA((N_RT,)),
            pltpu.SemaphoreType.DMA((N_RT,)),
        ],
        compiler_params=pltpu.CompilerParams(collective_id=collective_id, has_side_effects=True, vmem_limit_bytes=56 << 20),
        name=f"reduce_tok_{collective_id}",
    )(part)


SLOTS = 48


def dot(a, b, ca, cb, dtype=jnp.float32):
    return lax.dot_general(a, b, (((ca,), (cb,)), ((), ())), preferred_element_type=jnp.float32).astype(dtype)


def activation(gate, up, back, weights):
    sigma = jax.nn.sigmoid(gate)
    scaled = weights * (gate * sigma) * up
    weighted = weights * back
    gate_bar = weighted * up * sigma * (1.0 + gate * (1.0 - sigma))
    up_bar = weighted * gate * sigma
    return scaled.astype(jnp.bfloat16), gate_bar.astype(jnp.bfloat16), up_bar.astype(jnp.bfloat16)


def local(features, expert_rows, route_weight, gate_proj, up_proj, down_proj, out_grad):
    loops = lax.axis_size("loop")
    toks = lax.axis_size("tok")
    me = lax.axis_index("loop")
    tok = lax.axis_index("tok")
    experts, rows = expert_rows.shape
    held, width = features.shape
    panel = gate_proj.shape[2]
    share = rows // toks

    owner = expert_rows // held
    holder = jnp.arange(loops)
    starts = jnp.sum((owner[:, None, :] < holder[None, :, None]).astype(jnp.int32), axis=2)
    start_of = jnp.sum(jnp.where(owner[:, :, None] == holder, starts[:, None, :], 0), axis=2)
    slot = jnp.arange(rows)[None, :] - start_of
    place = owner * SLOTS + slot

    own = jnp.arange(held) + me * held
    hits = expert_rows[:, :, None] == own
    present = jnp.any(hits, axis=1)
    before = jnp.arange(held)[:, None] > jnp.arange(held)[None, :]
    rank = jnp.sum(jnp.where(before[None], present[:, None, :], False).astype(jnp.int32), axis=2)
    pick = (present[:, None, :] & (rank[:, None, :] == jnp.arange(SLOTS)[None, :, None])).astype(jnp.bfloat16)
    pick = pick.reshape(experts * SLOTS, held)
    both = jnp.concatenate([features, out_grad], axis=1)
    sent = dot(pick, both, 1, 0, jnp.bfloat16)

    everyone = gather_loop(sent.reshape(experts, SLOTS, 2 * width), 0)
    spread = (place[:, :, None] == jnp.arange(loops * SLOTS)).astype(jnp.bfloat16)
    compact = [
        dot(spread[e], everyone[:, e].reshape(loops * SLOTS, 2 * width), 1, 0, jnp.bfloat16)
        for e in range(experts)
    ]
    token_rows = [c[:, :width] for c in compact]
    grad_rows = [c[:, width:] for c in compact]

    parts = []
    for e in range(experts):
        three = [
            dot(token_rows[e], gate_proj[e], 1, 0),
            dot(token_rows[e], up_proj[e], 1, 0),
            dot(grad_rows[e], down_proj[e], 1, 1),
        ]
        parts.append(jnp.stack([p.reshape(toks, share, panel) for p in three], axis=1))
    hidden = jnp.stack(parts, axis=1).reshape(toks, experts, 3 * share, panel)
    hidden = reduce_tok(hidden, 1).reshape(experts, 3, share, panel)
    weights = lax.dynamic_slice_in_dim(route_weight, tok * share, share, axis=1)[:, :, None]
    acts = activation(hidden[:, 0], hidden[:, 1], hidden[:, 2], weights)
    acts = jnp.stack(acts, axis=1).reshape(experts, 3 * share, panel)
    acts = gather_tok(acts, 2).reshape(toks, experts, 3, share, panel)
    scaled, gate_bar, up_bar = (
        [acts[:, e, k].reshape(rows, panel) for e in range(experts)] for k in range(3)
    )

    out_part = jnp.concatenate([dot(scaled[e], down_proj[e], 1, 0) for e in range(experts)], axis=0)
    in_part = jnp.concatenate(
        [dot(gate_bar[e], gate_proj[e], 1, 1) + dot(up_bar[e], up_proj[e], 1, 1) for e in range(experts)],
        axis=0,
    )
    shape = (LAYERS, 2, 1, 2, experts * rows // loops, width)
    part = jnp.concatenate([out_part.reshape(shape), in_part.reshape(shape)], axis=2)
    summed = reduce_loop(part, 3).astype(jnp.bfloat16)
    summed = gather_loop(summed, 4).reshape(loops // 2, 2, 2, -1, width)
    home = (expert_rows.reshape(-1)[None, :] == own[:, None]).astype(jnp.bfloat16)
    mixed, feature_grad = (
        dot(home, summed[:, k].reshape(experts * rows, width), 1, 0, jnp.bfloat16) for k in range(2)
    )

    gate_grad = jnp.stack([dot(token_rows[e], gate_bar[e], 0, 0, jnp.bfloat16) for e in range(experts)])
    up_grad = jnp.stack([dot(token_rows[e], up_bar[e], 0, 0, jnp.bfloat16) for e in range(experts)])
    down_grad = jnp.stack([dot(scaled[e], grad_rows[e], 0, 0, jnp.bfloat16) for e in range(experts)])
    return (mixed, feature_grad, gate_grad, up_grad, down_grad)


def solution(mesh):
    placed = (
        P("loop", "tok"),
        P(),
        P(),
        P(None, "tok", "loop"),
        P(None, "tok", "loop"),
        P(None, "loop", "tok"),
        P("loop", "tok"),
    )
    return jax.shard_map(
        local,
        mesh=mesh,
        in_specs=placed,
        out_specs=(
            P("loop", "tok"),
            P("loop", "tok"),
            P(None, "tok", "loop"),
            P(None, "tok", "loop"),
            P(None, "loop", "tok"),
        ),
        check_vma=False,
    )
```

```python
import jax
import jax.numpy as jnp
from jax import lax
from jax.experimental import pallas as pl
from jax.experimental.pallas import tpu as pltpu

from jax.sharding import PartitionSpec as P

MESH = pl.DeviceIdType.MESH
ANY = pl.BlockSpec(memory_space=pl.ANY)
VM = pl.BlockSpec(memory_space=pltpu.VMEM)


def greet(peers):
    barrier = pltpu.get_barrier_semaphore()
    for peer in peers:
        pl.semaphore_signal(barrier, inc=1, device_id=peer, device_id_type=MESH)
    pl.semaphore_wait(barrier, len(peers))


class Sender:
    def __init__(self, send_sems, recv_sems):
        self.send_sems, self.recv_sems, self.copies = send_sems, recv_sems, []

    def start(self, src, dst, peer):
        k = len(self.copies)
        copy = pltpu.make_async_remote_copy(
            src_ref=src, dst_ref=dst, send_sem=self.send_sems.at[k], recv_sem=self.recv_sems.at[k],
            device_id=peer, device_id_type=MESH)
        copy.start()
        self.copies.append(copy)
        return copy

    def drain(self):
        for copy in self.copies:
            copy.wait_send()


def loop_place():
    me = lax.axis_index("loop")
    core = lax.rem(me, 2)
    side = lax.rem(me // 2, 2)
    layer = me // 4
    return layer, side, core


LAYERS = 8


def loop_index(layer, side, core):
    return lax.rem(layer + LAYERS, LAYERS) * 4 + side * 2 + core


def loop_peers(layer, side, core):
    return {
        "up": {"loop": loop_index(layer + 1, side, core)},
        "down": {"loop": loop_index(layer - 1, side, core)},
        "across": {"loop": loop_index(layer, 1 - side, core)},
        "twin": {"loop": loop_index(layer, side, 1 - core)},
    }


RUNS = {("own", 1): 3, ("own", -1): 4, ("mate", 1): 4, ("mate", -1): 3, ("q", 1): 4, ("q", -1): 3}


def gather_loop_body(src, dst, sender):
    layer, side, core = loop_place()
    other = 1 - side
    at = lambda d, s, c: loop_index(layer + d, s, c)
    peers = loop_peers(layer, side, core)
    own, mate = at(0, side, core), at(0, other, core)
    run, twins, crossed, order = {}, [], [], [(0, 0)]

    def step(kind, way, s, ref=None):
        half = 1 if kind == "q" else 0
        block = at(-way * (s - 1), other if kind == "mate" else side, core)
        ref = dst.at[half, block] if ref is None else ref
        run[kind, way, s] = sender.start(ref, dst.at[half, block], peers["up" if way == 1 else "down"])

    def double(half, block, ref=None):
        ref = dst.at[half, block] if ref is None else ref
        twins.append(sender.start(ref, dst.at[half, block], peers["twin"]))

    def relay():
        n = len(relayed)
        way, r = order[n]
        crossed[n].wait_recv()
        relayed.append(n)
        double(1, at(-way * r, other, core))

    relayed = []
    first = sender.start(src.at[0], dst.at[0, own], peers["across"])
    for way in (1, -1):
        step("q", way, 1, src.at[1])
        step("own", way, 1, src.at[0])
    for half in (0, 1):
        double(half, own, src.at[half])
    crossed.append(sender.start(src.at[1], dst.at[1, own], peers["across"]))
    first.wait_recv()
    for way in (1, -1):
        step("mate", way, 1)
    double(0, mate)
    for s in range(1, 5):
        for kind in ("q", "own", "mate"):
            for way in (1, -1):
                if s > RUNS[kind, way]:
                    continue
                run[kind, way, s].wait_recv()
                half = 1 if kind == "q" else 0
                block = at(-way * s, other if kind == "mate" else side, core)
                if s < RUNS[kind, way]:
                    step(kind, way, s + 1)
                if kind == "q":
                    crossed.append(sender.start(dst.at[1, block], dst.at[1, block], peers["across"]))
                    order.append((way, s))
                double(half, block)
        while len(relayed) < len(order) - 2:
            relay()
    while len(relayed) < len(order):
        relay()
    for copy in twins:
        copy.wait_recv()


N_LOOP = 21 + 1 + 8 + 32


def gather_loop_kernel(src, dst, send_sems, recv_sems, own_sems):
    place = loop_place()
    greet(tuple(loop_peers(*place).values()))
    own = loop_index(*place)
    keep = [pltpu.make_async_copy(src.at[h], dst.at[h, own], own_sems.at[h]) for h in (0, 1)]
    for copy in keep:
        copy.start()
    sender = Sender(send_sems, recv_sems)
    gather_loop_body(src, dst, sender)
    sender.drain()
    for copy in keep:
        copy.wait()


def gather_loop(block, collective_id, space=ANY):
    halves, rows, width = block.shape
    return pl.pallas_call(
        gather_loop_kernel,
        out_shape=jax.ShapeDtypeStruct((halves, 32, rows, width), block.dtype),
        in_specs=[VM],
        out_specs=space,
        scratch_shapes=[
            pltpu.SemaphoreType.DMA((N_LOOP,)),
            pltpu.SemaphoreType.DMA((N_LOOP,)),
            pltpu.SemaphoreType.DMA((2,)),
        ],
        compiler_params=pltpu.CompilerParams(collective_id=collective_id, has_side_effects=True),
        name=f"gather_loop_{collective_id}",
    )(block)


HOPS = {("own", 1): 4, ("own", -1): 3, ("mate", 1): 3, ("mate", -1): 4, ("q", 1): 4, ("q", -1): 3}
FAR_FIRST = (4, 3, -3, 2, -2, 1, -1, 0)


def reduce_loop_body(part, make, total, mail, crossing, landing, sender):
    layer, side, core = loop_place()
    other = 1 - side
    peers = loop_peers(layer, side, core)
    spot = lambda d: lax.rem(layer + d + LAYERS, LAYERS)
    twins, crossed, run, ready = {}, {}, {}, set()
    kinds = ("own", "mate", "q")

    def offer(d):
        make(spot(d))
        twins[d] = sender.start(part.at[spot(d), 1 - core], total.at[spot(d)], peers["twin"])

    def settle(d):
        twins[d].wait_recv()
        total[spot(d)] = total[spot(d)] + part[spot(d), core]
        crossed[d] = sender.start(total.at[spot(d), other, 1], crossing.at[FAR_FIRST.index(d)], peers["across"])

    def mine(kind, d):
        who = other if kind == "mate" else side
        return total.at[spot(d), who, 1 if kind == "q" else 0]

    def box(kind, way, j):
        return mail.at[kinds.index(kind), (0 if way == 1 else 1), j - 1]

    def blend(d):
        if d not in ready:
            ready.add(d)
            crossed[d].wait_recv()
            total[spot(d), side, 1] = total[spot(d), side, 1] + crossing[FAR_FIRST.index(d)]

    def send(kind, way, j):
        if j > HOPS[kind, way]:
            return
        d = way * j if j < 4 else 4
        if kind == "q":
            blend(d)
        src = mine(kind, d)
        if j < HOPS[kind, way]:
            run[kind, way, j + 1].wait_recv()
            held = box(kind, way, j + 1)
            held[...] = held[...] + src[...]
            src = held
        run[kind, way, j] = sender.start(src, box(kind, way, j), peers["up" if way == 1 else "down"])

    offer(4)
    offer(3)
    offer(-3)
    settle(4)
    for j in (4, 3, 2, 1):
        for way in (1, -1):
            send("own", way, j)
            send("mate", way, j)
            if j < 4:
                send("q", way, j + 1)
        if j > 2:
            offer(j - 2)
            offer(2 - j)
        elif j == 2:
            offer(0)
        if j > 1:
            settle(j - 1)
            settle(1 - j)
        else:
            settle(0)
    for way in (1, -1):
        send("q", way, 1)

    def arrived(kind):
        for way in (1, -1):
            run[kind, way, 1].wait_recv()
        return mine(kind, 0)[...] + box(kind, 1, 1)[...] + box(kind, -1, 1)[...]

    landing[0] = arrived("mate")
    last = sender.start(landing.at[0], landing.at[1], peers["across"])
    blend(0)
    own = arrived("own")
    q = arrived("q")
    last.wait_recv()
    return own + landing[1], q


N_SUM = 8 + 8 + 21 + 1


def finish_kernel(acts, gate_w, up_w, down_w, tokens, out, part, total, mail, crossing, landing, piece, everyone,
                  send_sems, recv_sems, send2, recv2, own_sems):
    layer, side, core = loop_place()
    greet(tuple(loop_peers(layer, side, core).values()))
    share = acts.shape[2] // 3
    bf16 = jnp.bfloat16

    def make(z):
        e, y = z // 4, lax.rem(z, 4)
        scaled, gate_bar, up_bar = (
            jnp.concatenate([acts[2 * y + h, e, pl.ds(k * share, share)] for h in (0, 1)], axis=0) for k in range(3)
        )
        mixed = mm(scaled, down_w[e], 1, 0)
        back = mm(gate_bar, gate_w[e], 1, 1) + mm(up_bar, up_w[e], 1, 1)
        part[z, 0] = mixed.reshape(part.shape[2:])
        part[z, 1] = back.reshape(part.shape[2:])

    sender = Sender(send_sems, recv_sems)
    p, q = reduce_loop_body(part, make, total, mail, crossing, landing, sender)
    piece[0] = p.astype(bf16)
    piece[1] = q.astype(bf16)
    own = loop_index(layer, side, core)
    keep = [pltpu.make_async_copy(piece.at[h], everyone.at[h, own], own_sems.at[h]) for h in (0, 1)]
    for copy in keep:
        copy.start()
    later = Sender(send2, recv2)
    gather_loop_body(piece, everyone, later)
    for copy in keep:
        copy.wait()
    held = out.shape[1]
    lanes = tokens[...]
    mine = lax.broadcasted_iota(jnp.int32, (held, lanes.shape[1]), 0) + own * held
    home = jnp.where(mine == lanes, 1.0, 0.0).astype(bf16)
    rows, width = everyone.shape[2:]
    for k in range(2):
        rows_k = jnp.concatenate(
            [everyone[h, 2 * n + k] for n in range(16) for h in (0, 1)], axis=0
        )
        out[k] = mm(home, rows_k, 1, 0).astype(bf16)
    sender.drain()
    later.drain()


def mm(a, b, ca, cb):
    return lax.dot_general(a, b, (((ca,), (cb,)), ((), ())), preferred_element_type=jnp.float32)


def finish(acts, gate_w, up_w, down_w, tokens, held, collective_id):
    width = down_w.shape[2]
    rows = tokens.shape[1] // 32
    f32, bf16 = jnp.float32, jnp.bfloat16
    piece = (2, rows, width)
    dma = pltpu.SemaphoreType.DMA
    return pl.pallas_call(
        finish_kernel,
        out_shape=jax.ShapeDtypeStruct((2, held, width), bf16),
        in_specs=[VM] * 5,
        out_specs=VM,
        scratch_shapes=[
            pltpu.VMEM((LAYERS, 2, 2) + piece, f32),
            pltpu.VMEM((LAYERS, 2) + piece, f32),
            pltpu.VMEM((3, 2, 4, rows, width), f32),
            pltpu.VMEM((LAYERS, rows, width), f32),
            pltpu.VMEM((2, rows, width), f32),
            pltpu.VMEM(piece, bf16),
            pltpu.VMEM((2, 32, rows, width), bf16),
            dma((N_SUM,)), dma((N_SUM,)), dma((N_LOOP,)), dma((N_LOOP,)), dma((2,)),
        ],
        compiler_params=pltpu.CompilerParams(collective_id=collective_id, has_side_effects=True, vmem_limit_bytes=56 << 20),
        name="finish",
    )(acts, gate_w, up_w, down_w, tokens)


def tok_place():
    layer, side, core = loop_place()
    tok = lax.axis_index("tok")
    tall, high = tok // 2, lax.rem(tok, 2)
    step = lambda d: lax.rem(tall + d + 4, 4) * 2 + high
    peers = {
        "up": {"tok": step(1)},
        "down": {"tok": step(-1)},
        "low": {"loop": loop_index(layer, 1 - side, core)},
        "cross": {"loop": loop_index(layer, 1 - side, core), "tok": tall * 2 + 1 - high},
    }
    return tall, high, peers


def gather_tok_body(src, dst, transit, sender, tall, high, peers, keep=None):
    half_rows = src.shape[1] // 2
    A, B = pl.ds(0, half_rows), pl.ds(half_rows, half_rows)
    at = lambda d, h: lax.rem(tall + d + 4, 4) * 2 + h
    other = 1 - high
    own, mate = at(0, high), at(0, other)
    sent = {}

    def hop(ref, n):
        sent["low", n] = sender.start(ref.at[A], transit.at[n, 0], peers["low"])
        sent["cross", n] = sender.start(ref.at[B], transit.at[n, 1], peers["cross"])

    def pass_on(n, d, half):
        sent["low", n].wait_recv()
        sent["to", n, 0] = sender.start(transit.at[n, 0], dst.at[at(d, high), half, A], peers["cross"])
        sent["cross", n].wait_recv()
        sent["to", n, 1] = sender.start(transit.at[n, 1], dst.at[at(d, other), half, B], peers["low"])

    def landed(n):
        sent["to", n, 0].wait_recv()
        sent["to", n, 1].wait_recv()

    def ring(kind, ref, h, half):
        sent[kind, 1] = sender.start(ref, dst.at[at(0, h), half], peers["up"])
        sent[kind, -1] = sender.start(ref, dst.at[at(0, h), half], peers["down"])

    def onward(kind, h, half):
        for way, piece, to in ((1, A, "up"), (-1, B, "down")):
            sent[kind, way].wait_recv()
            ref = dst.at[at(-way, h), half, piece]
            sent[kind, way, 2] = sender.start(ref, ref, peers[to])

    def closed(kind):
        sent[kind, 1, 2].wait_recv()
        sent[kind, -1, 2].wait_recv()

    hop(src.at[0], 0)
    ring("q", src.at[1], high, 1)
    ring("p", src.at[0], high, 0)
    hop(src.at[1], 1)
    pass_on(0, 0, 0)
    onward("q", high, 1)
    hop(dst.at[at(-1, high), 1], 2)
    hop(dst.at[at(1, high), 1], 3)
    landed(0)
    ring("m", dst.at[mate, 0], other, 0)
    pass_on(1, 0, 1)
    onward("p", high, 0)
    closed("q")
    hop(dst.at[at(2, high), 1], 4)
    pass_on(2, -1, 1)
    pass_on(3, 1, 1)
    onward("m", other, 0)
    pass_on(4, 2, 1)
    closed("p")
    closed("m")
    for n in range(1, 5):
        landed(n)


def reduce_tok_body(part, make, settled, post, mail, transit, landing, carry, sender, tall, high, peers):
    rows = part.shape[2]
    half_rows = rows // 2
    A, B = pl.ds(0, half_rows), pl.ds(half_rows, half_rows)
    at = lambda d, h: lax.rem(tall + d + 4, 4) * 2 + h
    other = 1 - high
    sent = {}
    f32, bf16 = jnp.float32, jnp.bfloat16

    def hop(n):
        sent["low", n] = sender.start(post.at[n, A], transit.at[n, 0], peers["low"])
        sent["cross", n] = sender.start(post.at[n, B], transit.at[n, 1], peers["cross"])

    def pass_on(n):
        sent["low", n].wait_recv()
        sent["to", n, 0] = sender.start(transit.at[n, 0], landing.at[n, A], peers["cross"])
        sent["cross", n].wait_recv()
        sent["to", n, 1] = sender.start(transit.at[n, 1], landing.at[n, B], peers["low"])

    def landed(n):
        sent["to", n, 0].wait_recv()
        sent["to", n, 1].wait_recv()

    def term(kind, d, rows_of):
        if kind == 2:
            return carry[DS.index(d), rows_of]
        return part[at(d, high if kind == 0 else other), 0, rows_of]

    def far(kind):
        for w, way, piece, to in ((0, 1, A, "up"), (1, -1, B, "down")):
            mail[kind, w, 0, piece] = term(kind, 2, piece).astype(bf16)
            sent[kind, way, 2] = sender.start(mail.at[kind, w, 0, piece], mail.at[kind, w, 1, piece], peers[to])

    def near(kind):
        for w, way, piece, rest, to in ((0, 1, A, B, "up"), (1, -1, B, A, "down")):
            mail[kind, w, 2, rest] = term(kind, way, rest).astype(bf16)
            sent[kind, way, 2].wait_recv()
            mail[kind, w, 2, piece] = (term(kind, way, piece) + mail[kind, w, 1, piece].astype(f32)).astype(bf16)
            sent[kind, way, 1] = sender.start(mail.at[kind, w, 2], mail.at[kind, w, 3], peers[to])

    def whole(kind):
        sent[kind, 1, 1].wait_recv()
        sent[kind, -1, 1].wait_recv()
        everything = pl.ds(0, rows)
        return term(kind, 0, everything) + mail[kind, 0, 3].astype(f32) + mail[kind, 1, 3].astype(f32)

    DS = (2, 1, -1, 0)
    make(0, 2)
    far(1)
    far(0)
    for n, d in enumerate(DS[:3]):
        make(1, d)
        post[n] = part[at(d, other), 1].astype(bf16)
        hop(n)
    make(0, 1)
    make(0, -1)
    near(1)
    pass_on(0)
    near(0)
    make(1, 0)
    post[3] = part[at(0, other), 1].astype(bf16)
    hop(3)
    pass_on(1)
    make(0, 0)
    pass_on(2)

    def mix(n):
        landed(n)
        carry[n] = part[at(DS[n], high), 1] + landing[n].astype(f32)

    mix(0)
    far(2)
    pass_on(3)
    post[4] = whole(1).astype(bf16)
    hop(4)
    mix(1)
    mix(2)
    near(2)
    pass_on(4)
    mix(3)
    own = whole(0)
    landed(4)
    settled(0, own + landing[4].astype(f32))
    settled(1, whole(2))


N_T = 5 * 4 + 3 * 4


def hidden_kernel(everyone, place, weight, gate_w, up_w, down_w, acts, rows_out, part, post, mail, transit, landing, carry,
                  turn, transit2, send_sems, recv_sems, send2, recv2, own_sem):
    tall, high, peers = tok_place()
    greet(tuple(peers.values()))
    bf16 = jnp.bfloat16
    width = gate_w.shape[1]
    share = part.shape[2] // 3
    pair = 2 * share
    slots = everyone.shape[1]

    def make(e, d):
        y = lax.rem(tall + d + 4, 4)
        start = pl.multiple_of(y * pair, pair)
        spread = place[e, pl.ds(start, pair)] == lax.broadcasted_iota(jnp.int32, (pair, slots), 1)
        rows = mm(jnp.where(spread, 1.0, 0.0).astype(bf16), everyone[e], 1, 0).astype(bf16)
        rows_out[e, pl.ds(start, pair)] = rows
        gate = mm(rows[:, :width], gate_w[e], 1, 0)
        up = mm(rows[:, :width], up_w[e], 1, 0)
        back = mm(rows[:, width:], down_w[e], 1, 1)
        for h in (0, 1):
            for k, value in enumerate((gate, up, back)):
                part[2 * y + h, e, pl.ds(k * share, share)] = value[h * share : (h + 1) * share]

    def settled(e, sums):
        gate, up, back = (sums[k * share : (k + 1) * share] for k in range(3))
        w = weight[e, pl.ds(pl.multiple_of((tall * 2 + high) * share, share), share)]
        sigma = jax.nn.sigmoid(gate)
        weighted = w * back
        turn[e, pl.ds(0, share)] = (w * (gate * sigma) * up).astype(bf16)
        turn[e, pl.ds(share, share)] = (weighted * up * sigma * (1.0 + gate * (1.0 - sigma))).astype(bf16)
        turn[e, pl.ds(2 * share, share)] = (weighted * gate * sigma).astype(bf16)

    sender = Sender(send_sems, recv_sems)
    reduce_tok_body(part, make, settled, post, mail, transit, landing, carry, sender, tall, high, peers)
    keep = pltpu.make_async_copy(turn, acts.at[tall * 2 + high], own_sem)
    keep.start()
    later = Sender(send2, recv2)
    gather_tok_body(turn, acts, transit2, later, tall, high, peers)
    sender.drain()
    later.drain()
    keep.wait()


def hidden(everyone, place, weight, gate_w, up_w, down_w, toks, collective_id):
    experts, width, panel = gate_w.shape
    total = place.shape[1]
    rows = 3 * total // toks
    f32, bf16 = jnp.float32, jnp.bfloat16
    dma = pltpu.SemaphoreType.DMA
    return pl.pallas_call(
        hidden_kernel,
        out_shape=(
            jax.ShapeDtypeStruct((toks, experts, rows, panel), bf16),
            jax.ShapeDtypeStruct((experts, total, 2 * width), bf16),
        ),
        in_specs=[VM] * 6,
        out_specs=(ANY, VM),
        scratch_shapes=[
            pltpu.VMEM((toks, experts, rows, panel), f32),
            pltpu.VMEM((5, rows, panel), bf16),
            pltpu.VMEM((3, 2, 4, rows, panel), bf16),
            pltpu.VMEM((5, 2, rows // 2, panel), bf16),
            pltpu.VMEM((5, rows, panel), bf16),
            pltpu.VMEM((4, rows, panel), f32),
            pltpu.VMEM((experts, rows, panel), bf16),
            pltpu.VMEM((5, 2, rows // 2, panel), bf16),
            dma((N_T,)), dma((N_T,)), dma((N_T,)), dma((N_T,)), dma,
        ],
        compiler_params=pltpu.CompilerParams(collective_id=collective_id, has_side_effects=True, vmem_limit_bytes=60 << 20),
        name="hidden",
    )(everyone, place, weight, gate_w, up_w, down_w)


SLOTS = 48


def dot(a, b, ca, cb, dtype=jnp.float32):
    return lax.dot_general(a, b, (((ca,), (cb,)), ((), ())), preferred_element_type=jnp.float32).astype(dtype)


def local(features, expert_rows, route_weight, gate_proj, up_proj, down_proj, out_grad):
    loops = lax.axis_size("loop")
    toks = lax.axis_size("tok")
    me = lax.axis_index("loop")
    experts, rows = expert_rows.shape
    held, width = features.shape
    panel = gate_proj.shape[2]
    share = rows // toks

    owner = expert_rows // held
    holder = jnp.arange(loops)
    starts = jnp.sum((owner[:, None, :] < holder[None, :, None]).astype(jnp.int32), axis=2)
    start_of = jnp.sum(jnp.where(owner[:, :, None] == holder, starts[:, None, :], 0), axis=2)
    slot = jnp.arange(rows)[None, :] - start_of
    place = owner * SLOTS + slot

    own = jnp.arange(held) + me * held
    hits = expert_rows[:, :, None] == own
    present = jnp.any(hits, axis=1)
    before = jnp.arange(held)[:, None] > jnp.arange(held)[None, :]
    rank = jnp.sum(jnp.where(before[None], present[:, None, :], False).astype(jnp.int32), axis=2)
    pick = (present[:, None, :] & (rank[:, None, :] == jnp.arange(SLOTS)[None, :, None])).astype(jnp.bfloat16)
    pick = pick.reshape(experts * SLOTS, held)
    both = jnp.concatenate([features, out_grad], axis=1)
    sent = dot(pick, both, 1, 0, jnp.bfloat16)

    everyone = gather_loop(sent.reshape(experts, SLOTS, 2 * width), 0)
    everyone = everyone.reshape(experts, loops * SLOTS, 2 * width)
    acts, compact = hidden(
        everyone, place[:, :, None], route_weight[:, :, None], gate_proj, up_proj, down_proj, toks, 1
    )
    result = finish(acts, gate_proj, up_proj, down_proj, expert_rows.reshape(1, -1), held, 2)
    mixed, feature_grad = result[0], result[1]

    acts = acts.reshape(toks, experts, 3, share, panel)
    scaled, gate_bar, up_bar = (
        [acts[:, e, k].reshape(rows, panel) for e in range(experts)] for k in range(3)
    )
    token_rows = [compact[e, :, :width] for e in range(experts)]
    grad_rows = [compact[e, :, width:] for e in range(experts)]
    gate_grad = jnp.stack([dot(token_rows[e], gate_bar[e], 0, 0, jnp.bfloat16) for e in range(experts)])
    up_grad = jnp.stack([dot(token_rows[e], up_bar[e], 0, 0, jnp.bfloat16) for e in range(experts)])
    down_grad = jnp.stack([dot(scaled[e], grad_rows[e], 0, 0, jnp.bfloat16) for e in range(experts)])
    return (mixed, feature_grad, gate_grad, up_grad, down_grad)


def solution(mesh):
    placed = (
        P("loop", "tok"),
        P(),
        P(),
        P(None, "tok", "loop"),
        P(None, "tok", "loop"),
        P(None, "loop", "tok"),
        P("loop", "tok"),
    )
    return jax.shard_map(
        local,
        mesh=mesh,
        in_specs=placed,
        out_specs=(
            P("loop", "tok"),
            P("loop", "tok"),
            P(None, "tok", "loop"),
            P(None, "tok", "loop"),
            P(None, "loop", "tok"),
        ),
        check_vma=False,
    )
```

```python
import heapq

import jax
import jax.numpy as jnp
from jax import lax
from jax.experimental import pallas as pl
from jax.experimental.pallas import tpu as pltpu
from jax.sharding import PartitionSpec as P

MESH = pl.DeviceIdType.MESH
ANY = pl.BlockSpec(memory_space=pl.ANY)
VM = pl.BlockSpec(memory_space=pltpu.VMEM)
SLOTS = 48
LAYERS = 8
FAR_FIRST = (4, 3, -3, 2, -2, 1, -1, 0)
COPIES = 320
RING = 64


class Sender:
    def __init__(self, send_sems, recv_sems):
        self.send_sems, self.recv_sems, self.copies, self.left = send_sems, recv_sems, [], 0
        self.used, self.spare = 0, []

    def slot(self):
        if self.spare:
            return self.spare.pop(0)
        self.used += 1
        return self.used - 1

    def start(self, src, dst, peer, slot=None):
        k = len(self.copies)
        if k >= RING:
            self.gone(k - RING)
        copy = pltpu.make_async_remote_copy(
            src_ref=src, dst_ref=dst, send_sem=self.send_sems.at[k % RING],
            recv_sem=self.recv_sems.at[self.slot() if slot is None else slot],
            device_id=peer, device_id_type=MESH)
        copy.start()
        copy.number = k
        self.copies.append(copy)
        return copy

    def gone(self, upto):
        while self.left <= upto:
            self.copies[self.left].wait_send()
            self.left += 1

    def all_landed(self, ref, slot, peer):
        pltpu.make_async_remote_copy(
            src_ref=ref, dst_ref=ref, send_sem=self.send_sems.at[0], recv_sem=self.recv_sems.at[slot],
            device_id=peer, device_id_type=MESH).wait_recv()

    def drain(self):
        self.gone(len(self.copies) - 1)


def mm(a, b, ca, cb):
    return lax.dot_general(a, b, (((ca,), (cb,)), ((), ())), preferred_element_type=jnp.float32)


class Agenda:
    def __init__(self):
        self.heap, self.count, self.now = [], 0, 0.0

    def add(self, chain, when):
        heapq.heappush(self.heap, (when, self.count, chain))
        self.count += 1

    def run(self):
        while self.heap:
            when, _, chain = heapq.heappop(self.heap)
            self.now = max(self.now, when)
            due = next(chain, None)
            if due is not None:
                self.add(chain, max(due, when))


def kernel(sent, lanes8, tokens, gate_hbm, up_hbm, down_hbm, out_m, out_f, gate_g, up_g, down_g,
           G, rows_of, part, post, mail, transit, landing, carry, sums, turn, acts, transit2,
           part2, total, box_p, box_q, crossing, joint, piece, everyone, staging, cols, gate_t, up_t, down_w, early,
           send_sems, recv_sems, own_sems, out_sems, in_sems):
    f32, bf16 = jnp.float32, jnp.bfloat16
    me, tok = lax.axis_index("loop"), lax.axis_index("tok")
    core, side, layer = lax.rem(me, 2), lax.rem(me // 2, 2), me // 4
    tall, high = tok // 2, lax.rem(tok, 2)
    far_side, far_high = 1 - side, 1 - high
    spot = lambda d: lax.rem(layer + d + LAYERS, LAYERS)
    at = lambda d, s: spot(d) * 4 + s * 2 + core
    tok_at = lambda d, h: lax.rem(tall + d + 4, 4) * 2 + h
    to = {
        "z+": {"loop": spot(1) * 4 + side * 2 + core},
        "z-": {"loop": spot(-1) * 4 + side * 2 + core},
        "low": {"loop": layer * 4 + far_side * 2 + core},
        "twin": {"loop": layer * 4 + side * 2 + 1 - core},
        "y+": {"tok": tok_at(1, high)},
        "y-": {"tok": tok_at(-1, high)},
        "cross": {"loop": layer * 4 + far_side * 2 + core, "tok": tall * 2 + far_high},
    }
    Z = {1: "z+", -1: "z-"}
    Y = {1: "y+", -1: "y-"}
    loads = [
        pltpu.make_async_copy(src, dst, in_sems.at[n])
        for n, (src, dst) in enumerate(((gate_hbm, gate_t), (up_hbm, up_t), (down_hbm, down_w)))
    ]
    for load in loads:
        load.start()
    barrier = pltpu.get_barrier_semaphore()
    for peer in to.values():
        pl.semaphore_signal(barrier, inc=1, device_id=peer, device_id_type=MESH)
    pl.semaphore_wait(barrier, len(to))

    sender = Sender(send_sems, recv_sems)
    agenda = Agenda()
    own_copies = []

    def keep(src, dst):
        copy = pltpu.make_async_copy(src, dst, own_sems.at[len(own_copies)])
        copy.start()
        own_copies.append(copy)
        return copy

    def spread_loop(src, view, lanes, due, whole):
        run, crossed, order = {}, [], [(0, 0)]
        twin_slot = sender.slot()
        hops = {("own", 1): 3, ("own", -1): 4, ("mate", 1): 4, ("mate", -1): 3, ("q", 1): 4, ("q", -1): 3}
        p = next((n for n, mode in enumerate(lanes) if mode == "P"), None)
        q = next((n for n, mode in enumerate(lanes) if mode == "Q"), None)
        lane = {"own": p, "mate": p, "q": q}
        kinds = [k for k in ("q", "own", "mate") if lane[k] is not None]
        own = at(0, side)

        def step(kind, way, s):
            n = lane[kind]
            block = at(-way * (s - 1), far_side if kind == "mate" else side)
            ref = src(n) if (s == 1 and kind != "mate") else view(n, block)
            run[kind, way, s] = sender.start(ref, view(n, block), to[Z[way]])

        def double(n, block, ref=None):
            sender.start(view(n, block) if ref is None else ref, view(n, block), to["twin"], twin_slot)

        kept = [keep(src(n), view(n, own)) for n in range(len(lanes))]
        if p is not None:
            first = sender.start(src(p), view(p, own), to["low"])
        for kind in kinds:
            if kind != "mate":
                for way in (1, -1):
                    step(kind, way, 1)
        for n in range(len(lanes)):
            double(n, own, src(n))
        if q is not None:
            crossed.append(sender.start(src(q), view(q, own), to["low"]))
        relayed = []

        def relay():
            n = len(relayed)
            way, r = order[n]
            crossed[n].wait_recv()
            relayed.append(n)
            double(q, at(-way * r, far_side))

        yield due[0]
        if p is not None:
            first.wait_recv()
            for way in (1, -1):
                step("mate", way, 1)
            double(p, at(0, far_side))
        for s in range(1, 5):
            yield due[s]
            for kind in kinds:
                for way in (1, -1):
                    if s > hops[kind, way]:
                        continue
                    run[kind, way, s].wait_recv()
                    block = at(-way * s, far_side if kind == "mate" else side)
                    if s < hops[kind, way]:
                        step(kind, way, s + 1)
                    if kind == "q":
                        crossed.append(sender.start(view(q, block), view(q, block), to["low"]))
                        order.append((way, s))
                    double(lane[kind], block)
            while q is not None and len(relayed) < len(order) - 2:
                relay()
        yield due[5]
        while q is not None and len(relayed) < len(order):
            relay()
        yield due[6]
        sender.all_landed(whole, twin_slot, to["twin"])
        for copy in kept:
            copy.wait()

    share = part.shape[2] // 3
    pair = 2 * share
    slots = 32 * SLOTS

    def make(e, d):
        y = lax.rem(tall + d + 4, 4)
        start = pl.multiple_of(y * pair, pair)
        place = cols[pl.ds(start, pair), pl.ds(e, 1)].astype(jnp.int32)
        spread = jnp.where(place == lax.broadcasted_iota(jnp.int32, (pair, slots), 1), 1.0, 0.0).astype(bf16)
        x, dy = (mm(spread, G[e, k].reshape(slots, G.shape[4]), 1, 0).astype(bf16) for k in (0, 1))
        rows_of[e, 0, pl.ds(start, pair)] = x
        rows_of[e, 1, pl.ds(start, pair)] = dy
        for k, value in enumerate((mm(x, gate_t[e], 1, 1), mm(x, up_t[e], 1, 1), mm(dy, down_w[e], 1, 1))):
            for h in (0, 1):
                part[2 * y + h, e, pl.ds(k * share, share)] = value[h * share : (h + 1) * share]

    rows = part.shape[2]
    p_rows = mail.shape[4]
    q_rows = rows - p_rows
    DS = (2, 1, -1, 0)

    class Ferry:
        def __init__(self, passage):
            self.passage, self.sent = passage, {}

        def cut(self, size):
            return pl.ds(0, size // 2), pl.ds(size // 2, size // 2)

        def hop(self, n, ref):
            size = ref.shape[0]
            first, second = self.cut(size)
            half = pl.ds(0, size // 2)
            self.sent[n, 0] = sender.start(ref.at[first], self.passage.at[n, 0, half], to["low"])
            self.sent[n, 1] = sender.start(ref.at[second], self.passage.at[n, 1, half], to["cross"])

        def pass_on(self, n, first_to, second_to, slot=None):
            size = first_to.shape[0]
            first, second = self.cut(size)
            half = pl.ds(0, size // 2)
            self.sent[n, 0].wait_recv()
            self.sent[n, 2] = sender.start(self.passage.at[n, 0, half], first_to.at[first], to["cross"], slot)
            self.sent[n, 1].wait_recv()
            self.sent[n, 3] = sender.start(self.passage.at[n, 1, half], second_to.at[second], to["low"], slot)

        def landed(self, n):
            self.sent[n, 2].wait_recv()
            self.sent[n, 3].wait_recv()

    def settled(e):
        gate, up, back = (sums[e, pl.ds(k * share, share)] for k in range(3))
        w = cols[pl.ds(pl.multiple_of(tok * share, share), share), pl.ds(2 + e, 1)]
        sigma = jax.nn.sigmoid(gate)
        weighted = w * back
        turn[e, pl.ds(0, share)] = (w * (gate * sigma) * up).astype(bf16)
        turn[e, pl.ds(share, share)] = (weighted * up * sigma * (1.0 + gate * (1.0 - sigma))).astype(bf16)
        turn[e, pl.ds(2 * share, share)] = (weighted * gate * sigma).astype(bf16)

    def sum_tok(e, T, f):
        ferry = Ferry(transit.at[e])
        sent_tok = {}
        sizes = {0: p_rows, 1: p_rows, 2: q_rows}
        QR = pl.ds(p_rows, q_rows)

        def term(kind, d, lo, size):
            if kind == 2:
                return carry[e, DS.index(d), pl.ds(lo, size)]
            return part[tok_at(d, high if kind == 0 else far_high), e, pl.ds(lo, size)]

        def ends(kind, w):
            half = sizes[kind] // 2
            return (0, half, half) if w == 0 else (half, 0, half)

        def far(kind):
            for w, way in ((0, 1), (1, -1)):
                lo, _, half = ends(kind, w)
                at_lo = pl.ds(lo, half)
                mail[e, kind, w, 0, at_lo] = term(kind, 2, lo, half).astype(bf16)
                sent_tok[kind, way, 2] = sender.start(
                    mail.at[e, kind, w, 0, at_lo], mail.at[e, kind, w, 1, at_lo], to[Y[way]])

        def near(kind):
            for w, way in ((0, 1), (1, -1)):
                lo, rest, half = ends(kind, w)
                whole_of = pl.ds(0, sizes[kind])
                mail[e, kind, w, 2, pl.ds(rest, half)] = term(kind, way, rest, half).astype(bf16)
                sent_tok[kind, way, 2].wait_recv()
                mail[e, kind, w, 2, pl.ds(lo, half)] = (
                    term(kind, way, lo, half) + mail[e, kind, w, 1, pl.ds(lo, half)].astype(f32)).astype(bf16)
                sent_tok[kind, way, 1] = sender.start(
                    mail.at[e, kind, w, 2, whole_of], mail.at[e, kind, w, 3, whole_of], to[Y[way]])

        def whole(kind):
            sent_tok[kind, 1, 1].wait_recv()
            sent_tok[kind, -1, 1].wait_recv()
            full = pl.ds(0, sizes[kind])
            return (term(kind, 0, 0, sizes[kind]) + mail[e, kind, 0, 3, full].astype(f32)
                    + mail[e, kind, 1, 3, full].astype(f32))

        def give(n):
            make(e, DS[n])
            post[e, n, pl.ds(0, q_rows)] = part[tok_at(DS[n], far_high), e, QR].astype(bf16)
            ferry.hop(n, post.at[e, n, pl.ds(0, q_rows)])

        def pass_on(n):
            spot_of = landing.at[e, n, pl.ds(0, p_rows if n == 4 else q_rows)]
            ferry.pass_on(n, spot_of, spot_of)

        def mix(n):
            ferry.landed(n)
            carry[e, n] = part[tok_at(DS[n], high), e, QR] + landing[e, n, pl.ds(0, q_rows)].astype(f32)

        yield T
        give(0)
        far(1)
        far(0)
        yield T + f * 1.5
        give(1)
        yield T + f * 2.8
        give(2)
        yield T + f * 4.8
        pass_on(0)
        yield T + f * 6.4
        near(1)
        near(0)
        give(3)
        yield T + f * 7.9
        pass_on(1)
        yield T + f * 8.5
        mix(0)
        far(2)
        yield T + f * 10.0
        pass_on(2)
        yield T + f * 12.0
        post[e, 4] = whole(1).astype(bf16)
        ferry.hop(4, post.at[e, 4])
        mix(1)
        yield T + f * 13.0
        pass_on(3)
        yield T + f * 14.0
        mix(2)
        near(2)
        yield T + f * 16.0
        sums[e, pl.ds(0, p_rows)] = whole(0)
        pass_on(4)
        yield T + f * 17.5
        mix(3)
        yield T + f * 19.0
        sums[e, QR] = whole(2)
        yield T + f * 20.0
        ferry.landed(4)
        sums[e, pl.ds(0, p_rows)] = sums[e, pl.ds(0, p_rows)] + landing[e, 4].astype(f32)
        settled(e)

    def spread_tok(e, U, f):
        ferry = Ferry(transit2.at[e])
        sent_back = {}
        part_of = {"p": (0, p_rows), "m": (0, p_rows), "q": (p_rows, q_rows)}
        PR, QR = pl.ds(0, p_rows), pl.ds(p_rows, q_rows)
        side_of = {"p": high, "m": far_high, "q": high}

        def ring(kind, ref):
            lo, size = part_of[kind]
            for way in (1, -1):
                sent_back[kind, way] = sender.start(
                    ref, acts.at[tok_at(0, side_of[kind]), e, pl.ds(lo, size)], to[Y[way]])

        def onward(kind):
            lo, size = part_of[kind]
            for way, start in ((1, lo), (-1, lo + size // 2)):
                sent_back[kind, way].wait_recv()
                ref = acts.at[tok_at(-way, side_of[kind]), e, pl.ds(start, size // 2)]
                sent_back[kind, way, 2] = sender.start(ref, ref, to[Y[way]], None if kind == "q" else ring_slot)

        def closed(kind):
            sent_back[kind, 1, 2].wait_recv()
            sent_back[kind, -1, 2].wait_recv()

        def pass_on(n, d, which):
            ferry.pass_on(n, acts.at[tok_at(d, high), e, which], acts.at[tok_at(d, far_high), e, which],
                          last_slot if n else None)

        last_slot, ring_slot = sender.slot(), sender.slot()
        mine = acts.at[tok_at(0, high), e]
        kept = keep(turn.at[e], mine)
        ferry.hop(0, turn.at[e, PR])
        ring("q", turn.at[e, QR])
        ring("p", turn.at[e, PR])
        ferry.hop(1, turn.at[e, QR])
        yield U + f * 4.0
        pass_on(0, 0, PR)
        yield U + f * 4.6
        onward("q")
        ferry.hop(2, acts.at[tok_at(-1, high), e, QR])
        ferry.hop(3, acts.at[tok_at(1, high), e, QR])
        yield U + f * 6.5
        pass_on(1, 0, QR)
        yield U + f * 7.5
        ferry.landed(0)
        ring("m", acts.at[tok_at(0, far_high), e, PR])
        onward("p")
        yield U + f * 8.5
        closed("q")
        ferry.hop(4, acts.at[tok_at(2, high), e, QR])
        yield U + f * 9.5
        pass_on(2, -1, QR)
        yield U + f * 12.0
        pass_on(3, 1, QR)
        yield U + f * 13.0
        onward("m")
        yield U + f * 14.5
        pass_on(4, 2, QR)
        yield U + f * 16.0
        sender.all_landed(acts.at[pl.ds(0, 2), e, PR], ring_slot, to["y+"])
        yield U + f * 18.0
        sender.all_landed(acts.at[pl.ds(0, 4), e, QR], last_slot, to["cross"])
        kept.wait()

    def product(e, z):
        scaled, gate_bar, up_bar = (acts[z, e, pl.ds(k * share, share)] for k in range(3))
        part2[z, 0] = mm(scaled, down_w[e], 1, 0).reshape(part2.shape[2:])
        part2[z, 1] = (mm(gate_bar, gate_t[e], 1, 0) + mm(up_bar, up_t[e], 1, 0)).reshape(part2.shape[2:])

    last_offers, unsettled = [], set()

    def sum_loop(e, lanes, result, start, due):
        twins, crossed, run, ready = {}, {}, {}, set()
        hops = {("own", 1): 4, ("own", -1): 3, ("mate", 1): 3, ("mate", -1): 4, ("q", 1): 4, ("q", -1): 3}
        p, q = lanes.get("P"), lanes.get("Q")
        kinds = (["own", "mate"] if p else []) + (["q"] if q else [])
        yield start
        while unsettled:
            start += 0.5
            yield start
        for copy in last_offers:
            sender.gone(copy.number)
        last_offers.clear()
        unsettled.update(FAR_FIRST)

        def offer(d):
            product(e, spot(d))
            twins[d] = sender.start(part2.at[spot(d), 1 - core], total.at[e, spot(d)], to["twin"])
            last_offers.append(twins[d])

        def settle(d):
            unsettled.remove(d)
            twins[d].wait_recv()
            total[e, spot(d)] = total[e, spot(d)] + part2[spot(d), core]
            if q:
                crossed[d] = sender.start(
                    total.at[e, spot(d), far_side, q], crossing.at[e, FAR_FIRST.index(d), pl.ds(0, q.size)], to["low"])

        def mine(kind, d):
            return total.at[e, spot(d), far_side if kind == "mate" else side, q if kind == "q" else p]

        def box(kind, way, j):
            w = 0 if way == 1 else 1
            if kind == "q":
                return box_q.at[e, w, j - 1, pl.ds(0, q.size)]
            return box_p.at[e, 0 if kind == "own" else 1, w, j - 1, pl.ds(0, p.size)]

        def blend(d):
            if d not in ready:
                ready.add(d)
                crossed[d].wait_recv()
                total[e, spot(d), side, q] = (
                    total[e, spot(d), side, q] + crossing[e, FAR_FIRST.index(d), pl.ds(0, q.size)])

        def send(kind, way, j):
            if j > hops[kind, way]:
                return
            d = way * j if j < 4 else 4
            if kind == "q":
                blend(d)
            src = mine(kind, d)
            if j < hops[kind, way]:
                run[kind, way, j + 1].wait_recv()
                held = box(kind, way, j + 1)
                held[...] = held[...] + src[...]
                src = held
            run[kind, way, j] = sender.start(src, box(kind, way, j), to[Z[way]])

        for n, d in enumerate((4, 3, -3)):
            offer(d)
            yield start + 0.4 * n
        settle(4)
        for j in (4, 3, 2, 1):
            for kind in kinds:
                for way in (1, -1):
                    if kind != "q":
                        send(kind, way, j)
                    elif j < 4:
                        send(kind, way, j + 1)
            if j > 2:
                offer(j - 2)
                offer(2 - j)
            elif j == 2:
                offer(0)
            yield due[4 - j]
            for d in ((j - 1, 1 - j) if j > 1 else (0,)):
                settle(d)
        if q:
            for way in (1, -1):
                send("q", way, 1)
        yield due[4]

        def arrived(kind):
            for way in (1, -1):
                run[kind, way, 1].wait_recv()
            return mine(kind, 0)[...] + box(kind, 1, 1)[...] + box(kind, -1, 1)[...]

        if p:
            joint[e, 0, pl.ds(0, p.size)] = arrived("mate")
            last = sender.start(joint.at[e, 0, pl.ds(0, p.size)], joint.at[e, 1, pl.ds(0, p.size)], to["low"])
            own = arrived("own")
        if q:
            blend(0)
            piece[result, q] = arrived("q").astype(bf16)
        yield due[5]
        if p:
            last.wait_recv()
            piece[result, p] = (own + joint[e, 1, pl.ds(0, p.size)]).astype(bf16)

    def weight_grads(e):
        acts_of = lambda k: jnp.concatenate([acts[t, e, pl.ds(k * share, share)] for t in range(8)], axis=0)
        for n, (k, arr, dst) in enumerate(((1, 0, gate_g), (2, 0, up_g), (0, 1, down_g))):
            staging[n, e] = mm(acts_of(k), rows_of[e, arr], 0, 0).astype(bf16)
            copy = pltpu.make_async_copy(staging.at[n, e], dst.at[e], out_sems.at[n, e])
            copy.start()
            out_copies.append(copy)
            yield agenda.now + 3.0

    out_copies = []

    def gather_in(e, due):
        return spread_loop(lambda n: sent.at[e, n], lambda n, block: G.at[e, n, block], ("P", "Q"), due, G.at[e, 0])

    def chain(e):
        start = (0.0, 12.0)[e]
        yield from gather_in(e, tuple(start + t for t in ((3, 4, 8, 12, 16, 19, 21), (3, 7, 11, 15, 19.5, 23, 25))[e]))
        if e == 0:
            for load in loads:
                load.wait()
        yield from sum_tok(e, (22.0, 38.0)[e], (1.3, 1.6)[e])
        yield from spread_tok(e, (50.0, 73.0)[e], 1.5)
        agenda.add(weight_grads(e), agenda.now + 3.0)
        S = (80.0, 102.0)[e]
        yield from sum_loop(e, {"P": pl.ds(0, SLOTS // 2), "Q": pl.ds(SLOTS // 2, SLOTS // 2)}, e, S,
                            tuple(S + t for t in (3.5, 8.5, 13.5, 17.5, 20, 23)))
        R = (106.0, 127.0)[e]
        yield from spread_loop(lambda n: piece.at[e], lambda n, block: everyone.at[e, block], ("PQ"[e],),
                               tuple(R + t for t in ((4, 8, 12, 16, 20, 22, 24), (2.5, 4.5, 7, 9.5, 12, 13, 14))[e]),
                               everyone.at[e, pl.ds(0, 16)])
        partial_result(e)

    held = out_m.shape[0]

    def partial_result(e):
        lanes = tokens[pl.ds(e, 1)]
        mine = lax.broadcasted_iota(jnp.int32, (held, lanes.shape[1]), 0) + me * held
        home = jnp.where(mine == lanes, 1.0, 0.0).astype(bf16)
        for k, dst in enumerate((out_m, out_f)):
            found = jnp.concatenate([everyone[e, 2 * n + k] for n in range(16)], axis=0)
            value = mm(home, found, 1, 0)
            if e == 0:
                early[k] = value
            else:
                dst[...] = (early[k] + value).astype(bf16)

    def columns():
        cols[...] = jnp.transpose(jnp.concatenate([lanes8[...], jnp.zeros((120, cols.shape[0]), f32)], axis=0))
        yield

    agenda.add(chain(0), 0.0)
    agenda.add(columns(), 2.0)
    agenda.add(chain(1), 12.0)
    agenda.run()

    sender.drain()
    for copy in out_copies:
        copy.wait()


def everything(sent, lanes8, tokens, gate_t, up_t, down_w, held):
    experts, panel, width = down_w.shape
    total = lanes8.shape[1]
    toks = 8
    rows = 3 * total // toks
    p_rows = 160
    q_rows = rows - p_rows
    f32, bf16 = jnp.float32, jnp.bfloat16
    dma = pltpu.SemaphoreType.DMA
    V = pltpu.VMEM
    grads = jax.ShapeDtypeStruct((experts, panel, width), bf16)
    return pl.pallas_call(
        kernel,
        out_shape=(jax.ShapeDtypeStruct((held, width), bf16),) * 2 + (grads,) * 3,
        in_specs=[VM] * 3 + [ANY] * 3,
        out_specs=(VM, VM, ANY, ANY, ANY),
        scratch_shapes=[
            V((experts, 2, 32, SLOTS, width), bf16),
            V((experts, 2, total, width), bf16),
            V((toks, experts, rows, panel), f32),
            V((experts, 5, p_rows, panel), bf16),
            V((experts, 3, 2, 4, p_rows, panel), bf16),
            V((experts, 5, 2, p_rows // 2, panel), bf16),
            V((experts, 5, p_rows, panel), bf16),
            V((experts, 4, q_rows, panel), f32),
            V((experts, rows, panel), f32),
            V((experts, rows, panel), bf16),
            V((toks, experts, rows, panel), bf16),
            V((experts, 5, 2, p_rows // 2, panel), bf16),
            V((LAYERS, 2, 2, SLOTS, width), f32),
            V((experts, LAYERS, 2, SLOTS, width), f32),
            V((experts, 2, 2, 4, SLOTS // 2, width), f32),
            V((experts, 2, 4, SLOTS // 2, width), f32),
            V((experts, LAYERS, SLOTS // 2, width), f32),
            V((experts, 2, SLOTS // 2, width), f32),
            V((experts, SLOTS, width), bf16),
            V((experts, 32, SLOTS, width), bf16),
            V((3, experts, panel, width), bf16),
            V((total, 128), f32),
            V((experts, panel, width), bf16), V((experts, panel, width), bf16), V((experts, panel, width), bf16),
            V((2, held, width), f32),
            dma((RING,)), dma((COPIES,)), dma((12,)), dma((3, experts)), dma((3,)),
        ],
        compiler_params=pltpu.CompilerParams(
            collective_id=0, has_side_effects=True, vmem_limit_bytes=67_043_328),
        name="everything",
    )(sent, lanes8, tokens, gate_t, up_t, down_w)


def hand_over_kernel(*refs):
    n = len(refs) // 2
    for src, dst in zip(refs[:n], refs[n:]):
        dst[...] = src[...]


def hand_over(*arrays):
    return pl.pallas_call(
        hand_over_kernel,
        out_shape=tuple(jax.ShapeDtypeStruct(a.shape, a.dtype) for a in arrays),
        in_specs=[VM] * len(arrays),
        out_specs=(VM,) * len(arrays),
        name="hand_over",
    )(*arrays)


def local(features, expert_rows, route_weight, gate_proj, up_proj, down_proj, out_grad):
    loops = lax.axis_size("loop")
    me = lax.axis_index("loop")
    experts, rows = expert_rows.shape
    held, width = features.shape

    owner = expert_rows // held
    holder = jnp.arange(loops)
    starts = jnp.sum((owner[:, None, :] < holder[None, :, None]).astype(jnp.int32), axis=2)
    start_of = jnp.sum(jnp.where(owner[:, :, None] == holder, starts[:, None, :], 0), axis=2)
    place = owner * SLOTS + jnp.arange(rows)[None, :] - start_of
    lanes8 = jnp.concatenate([place.astype(jnp.float32), route_weight, jnp.zeros((4, rows), jnp.float32)], axis=0)

    own = jnp.arange(held) + me * held
    present = jnp.any(expert_rows[:, :, None] == own, axis=1)
    before = jnp.arange(held)[:, None] > jnp.arange(held)[None, :]
    rank = jnp.sum(jnp.where(before[None], present[:, None, :], False).astype(jnp.int32), axis=2)
    pick = (present[:, None, :] & (rank[:, None, :] == jnp.arange(SLOTS)[None, :, None])).astype(jnp.bfloat16)
    pick = pick.reshape(experts * SLOTS, held)
    sent = jnp.stack(
        [mm(pick, v, 1, 0).astype(jnp.bfloat16).reshape(experts, SLOTS, width) for v in (features, out_grad)], axis=1
    )
    mixed, feature_grad, gate_grad, up_grad, down_grad = everything(
        sent, lanes8, expert_rows, jnp.swapaxes(gate_proj, 1, 2), jnp.swapaxes(up_proj, 1, 2),
        down_proj, held)
    mixed, feature_grad, gate_grad, up_grad, down_grad = hand_over(mixed, feature_grad, gate_grad, up_grad, down_grad)
    return (mixed, feature_grad, jnp.swapaxes(gate_grad, 1, 2), jnp.swapaxes(up_grad, 1, 2), down_grad)


def solution(mesh):
    placed = (
        P("loop", "tok"),
        P(),
        P(),
        P(None, "tok", "loop"),
        P(None, "tok", "loop"),
        P(None, "loop", "tok"),
        P("loop", "tok"),
    )
    return jax.shard_map(
        local,
        mesh=mesh,
        in_specs=placed,
        out_specs=(
            P("loop", "tok"),
            P("loop", "tok"),
            P(None, "tok", "loop"),
            P(None, "tok", "loop"),
            P(None, "loop", "tok"),
        ),
        check_vma=False,
    )
```

```python
import heapq

import jax
import jax.numpy as jnp
from jax import lax
from jax.experimental import pallas as pl
from jax.experimental.pallas import tpu as pltpu
from jax.sharding import PartitionSpec as P

MESH = pl.DeviceIdType.MESH
ANY = pl.BlockSpec(memory_space=pl.ANY)
VM = pl.BlockSpec(memory_space=pltpu.VMEM)
SLOTS = 48
LAYERS = 8
FAR_FIRST = (4, 3, -3, 2, -2, 1, -1, 0)
COPIES = 320
RING = 64


class Sender:
    def __init__(self, send_sems, recv_sems):
        self.send_sems, self.recv_sems, self.copies, self.left = send_sems, recv_sems, [], 0
        self.used, self.spare = 0, []

    def slot(self):
        if self.spare:
            return self.spare.pop(0)
        self.used += 1
        return self.used - 1

    def start(self, src, dst, peer, slot=None):
        k = len(self.copies)
        if k >= RING:
            self.gone(k - RING)
        copy = pltpu.make_async_remote_copy(
            src_ref=src, dst_ref=dst, send_sem=self.send_sems.at[k % RING],
            recv_sem=self.recv_sems.at[self.slot() if slot is None else slot],
            device_id=peer, device_id_type=MESH)
        copy.start()
        copy.number = k
        self.copies.append(copy)
        return copy

    def gone(self, upto):
        while self.left <= upto:
            self.copies[self.left].wait_send()
            self.left += 1

    def all_landed(self, ref, slot, peer):
        pltpu.make_async_remote_copy(
            src_ref=ref, dst_ref=ref, send_sem=self.send_sems.at[0], recv_sem=self.recv_sems.at[slot],
            device_id=peer, device_id_type=MESH).wait_recv()

    def drain(self):
        self.gone(len(self.copies) - 1)


def mm(a, b, ca, cb):
    return lax.dot_general(a, b, (((ca,), (cb,)), ((), ())), preferred_element_type=jnp.float32)


class Agenda:
    def __init__(self):
        self.heap, self.count, self.now = [], 0, 0.0

    def add(self, chain, when):
        heapq.heappush(self.heap, (when, self.count, chain))
        self.count += 1

    def run(self):
        while self.heap:
            when, _, chain = heapq.heappop(self.heap)
            self.now = max(self.now, when)
            due = next(chain, None)
            if due is not None:
                self.add(chain, max(due, when))


def kernel(sent, place_of, weight_of, tokens, gate_hbm, up_hbm, down_hbm, out_m, out_f, gate_g, up_g, down_g,
           G, rows_of, part, post, mail, transit, landing, carry, sums, turn, acts, transit2,
           part2, total, box_p, box_q, crossing, joint, piece, everyone, staging, cols, gate_t, up_t, down_w, early,
           send_sems, recv_sems, own_sems, out_sems, in_sems):
    f32, bf16 = jnp.float32, jnp.bfloat16
    me, tok = lax.axis_index("loop"), lax.axis_index("tok")
    core, side, layer = lax.rem(me, 2), lax.rem(me // 2, 2), me // 4
    tall, high = tok // 2, lax.rem(tok, 2)
    far_side, far_high = 1 - side, 1 - high
    spot = lambda d: lax.rem(layer + d + LAYERS, LAYERS)
    at = lambda d, s: spot(d) * 4 + s * 2 + core
    tok_at = lambda d, h: lax.rem(tall + d + 4, 4) * 2 + h
    to = {
        "z+": {"loop": spot(1) * 4 + side * 2 + core},
        "z-": {"loop": spot(-1) * 4 + side * 2 + core},
        "low": {"loop": layer * 4 + far_side * 2 + core},
        "twin": {"loop": layer * 4 + side * 2 + 1 - core},
        "y+": {"tok": tok_at(1, high)},
        "y-": {"tok": tok_at(-1, high)},
        "cross": {"loop": layer * 4 + far_side * 2 + core, "tok": tall * 2 + far_high},
    }
    Z = {1: "z+", -1: "z-"}
    Y = {1: "y+", -1: "y-"}
    loads = [
        pltpu.make_async_copy(src, dst, in_sems.at[n])
        for n, (src, dst) in enumerate(((gate_hbm, gate_t), (up_hbm, up_t), (down_hbm, down_w)))
    ]
    for load in loads:
        load.start()
    barrier = pltpu.get_barrier_semaphore()
    for peer in to.values():
        pl.semaphore_signal(barrier, inc=1, device_id=peer, device_id_type=MESH)
    pl.semaphore_wait(barrier, len(to))

    sender = Sender(send_sems, recv_sems)
    agenda = Agenda()
    own_copies = []

    def keep(src, dst):
        copy = pltpu.make_async_copy(src, dst, own_sems.at[len(own_copies)])
        copy.start()
        own_copies.append(copy)
        return copy

    def spread_loop(src, view, lanes, due, whole):
        run, crossed, order = {}, [], [(0, 0)]
        twin_slot = sender.slot()
        hops = {("own", 1): 3, ("own", -1): 4, ("mate", 1): 4, ("mate", -1): 3, ("q", 1): 4, ("q", -1): 3}
        p = next((n for n, mode in enumerate(lanes) if mode == "P"), None)
        q = next((n for n, mode in enumerate(lanes) if mode == "Q"), None)
        lane = {"own": p, "mate": p, "q": q}
        kinds = [k for k in ("q", "own", "mate") if lane[k] is not None]
        own = at(0, side)

        def step(kind, way, s):
            n = lane[kind]
            block = at(-way * (s - 1), far_side if kind == "mate" else side)
            ref = src(n) if (s == 1 and kind != "mate") else view(n, block)
            run[kind, way, s] = sender.start(ref, view(n, block), to[Z[way]])

        def double(n, block, ref=None):
            sender.start(view(n, block) if ref is None else ref, view(n, block), to["twin"], twin_slot)

        kept = [keep(src(n), view(n, own)) for n in range(len(lanes))]
        if p is not None:
            first = sender.start(src(p), view(p, own), to["low"])
        for kind in kinds:
            if kind != "mate":
                for way in (1, -1):
                    step(kind, way, 1)
        for n in range(len(lanes)):
            double(n, own, src(n))
        if q is not None:
            crossed.append(sender.start(src(q), view(q, own), to["low"]))
        relayed = []

        def relay():
            n = len(relayed)
            way, r = order[n]
            crossed[n].wait_recv()
            relayed.append(n)
            double(q, at(-way * r, far_side))

        yield due[0]
        if p is not None:
            first.wait_recv()
            for way in (1, -1):
                step("mate", way, 1)
            double(p, at(0, far_side))
        for s in range(1, 5):
            yield due[s]
            for kind in kinds:
                for way in (1, -1):
                    if s > hops[kind, way]:
                        continue
                    run[kind, way, s].wait_recv()
                    block = at(-way * s, far_side if kind == "mate" else side)
                    if s < hops[kind, way]:
                        step(kind, way, s + 1)
                    if kind == "q":
                        crossed.append(sender.start(view(q, block), view(q, block), to["low"]))
                        order.append((way, s))
                    double(lane[kind], block)
            while q is not None and len(relayed) < len(order) - 2:
                relay()
        yield due[5]
        while q is not None and len(relayed) < len(order):
            relay()
        yield due[6]
        sender.all_landed(whole, twin_slot, to["twin"])
        for copy in kept:
            copy.wait()

    share = part.shape[2] // 3
    pair = 2 * share
    slots = 32 * SLOTS

    def make(e, d):
        y = lax.rem(tall + d + 4, 4)
        start = pl.multiple_of(y * pair, pair)
        place = cols[pl.ds(start, pair), pl.ds(e, 1)].astype(jnp.int32)
        spread = jnp.where(place == lax.broadcasted_iota(jnp.int32, (pair, slots), 1), 1.0, 0.0).astype(bf16)
        x, dy = (mm(spread, G[e, k].reshape(slots, G.shape[4]), 1, 0).astype(bf16) for k in (0, 1))
        rows_of[e, 0, pl.ds(start, pair)] = x
        rows_of[e, 1, pl.ds(start, pair)] = dy
        for k, value in enumerate((mm(x, gate_t[e], 1, 1), mm(x, up_t[e], 1, 1), mm(dy, down_w[e], 1, 1))):
            for h in (0, 1):
                part[2 * y + h, e, pl.ds(k * share, share)] = value[h * share : (h + 1) * share]

    rows = part.shape[2]
    p_rows = mail.shape[4]
    q_rows = rows - p_rows
    DS = (2, 1, -1, 0)

    class Ferry:
        def __init__(self, passage):
            self.passage, self.sent = passage, {}

        def cut(self, size):
            return pl.ds(0, size // 2), pl.ds(size // 2, size // 2)

        def hop(self, n, ref):
            size = ref.shape[0]
            first, second = self.cut(size)
            half = pl.ds(0, size // 2)
            self.sent[n, 0] = sender.start(ref.at[first], self.passage.at[n, 0, half], to["low"])
            self.sent[n, 1] = sender.start(ref.at[second], self.passage.at[n, 1, half], to["cross"])

        def pass_on(self, n, first_to, second_to, slot=None):
            size = first_to.shape[0]
            first, second = self.cut(size)
            half = pl.ds(0, size // 2)
            self.sent[n, 0].wait_recv()
            self.sent[n, 2] = sender.start(self.passage.at[n, 0, half], first_to.at[first], to["cross"], slot)
            self.sent[n, 1].wait_recv()
            self.sent[n, 3] = sender.start(self.passage.at[n, 1, half], second_to.at[second], to["low"], slot)

        def landed(self, n):
            self.sent[n, 2].wait_recv()
            self.sent[n, 3].wait_recv()

    def settled(e):
        gate, up, back = (sums[e, pl.ds(k * share, share)] for k in range(3))
        w = cols[pl.ds(pl.multiple_of(tok * share, share), share), pl.ds(2 + e, 1)]
        sigma = jax.nn.sigmoid(gate)
        weighted = w * back
        turn[e, pl.ds(0, share)] = (w * (gate * sigma) * up).astype(bf16)
        turn[e, pl.ds(share, share)] = (weighted * up * sigma * (1.0 + gate * (1.0 - sigma))).astype(bf16)
        turn[e, pl.ds(2 * share, share)] = (weighted * gate * sigma).astype(bf16)

    def sum_tok(e, T, f):
        ferry = Ferry(transit.at[e])
        sent_tok = {}
        sizes = {0: p_rows, 1: p_rows, 2: q_rows}
        QR = pl.ds(p_rows, q_rows)

        def term(kind, d, lo, size):
            if kind == 2:
                return carry[e, DS.index(d), pl.ds(lo, size)]
            return part[tok_at(d, high if kind == 0 else far_high), e, pl.ds(lo, size)]

        def ends(kind, w):
            half = sizes[kind] // 2
            return (0, half, half) if w == 0 else (half, 0, half)

        def far(kind):
            for w, way in ((0, 1), (1, -1)):
                lo, _, half = ends(kind, w)
                at_lo = pl.ds(lo, half)
                mail[e, kind, w, 0, at_lo] = term(kind, 2, lo, half).astype(bf16)
                sent_tok[kind, way, 2] = sender.start(
                    mail.at[e, kind, w, 0, at_lo], mail.at[e, kind, w, 1, at_lo], to[Y[way]])

        def near(kind):
            for w, way in ((0, 1), (1, -1)):
                lo, rest, half = ends(kind, w)
                whole_of = pl.ds(0, sizes[kind])
                mail[e, kind, w, 2, pl.ds(rest, half)] = term(kind, way, rest, half).astype(bf16)
                sent_tok[kind, way, 2].wait_recv()
                mail[e, kind, w, 2, pl.ds(lo, half)] = (
                    term(kind, way, lo, half) + mail[e, kind, w, 1, pl.ds(lo, half)].astype(f32)).astype(bf16)
                sent_tok[kind, way, 1] = sender.start(
                    mail.at[e, kind, w, 2, whole_of], mail.at[e, kind, w, 3, whole_of], to[Y[way]])

        def whole(kind):
            sent_tok[kind, 1, 1].wait_recv()
            sent_tok[kind, -1, 1].wait_recv()
            full = pl.ds(0, sizes[kind])
            return (term(kind, 0, 0, sizes[kind]) + mail[e, kind, 0, 3, full].astype(f32)
                    + mail[e, kind, 1, 3, full].astype(f32))

        def give(n):
            make(e, DS[n])
            post[e, n, pl.ds(0, q_rows)] = part[tok_at(DS[n], far_high), e, QR].astype(bf16)
            ferry.hop(n, post.at[e, n, pl.ds(0, q_rows)])

        def pass_on(n):
            spot_of = landing.at[e, n, pl.ds(0, p_rows if n == 4 else q_rows)]
            ferry.pass_on(n, spot_of, spot_of)

        def mix(n):
            ferry.landed(n)
            carry[e, n] = part[tok_at(DS[n], high), e, QR] + landing[e, n, pl.ds(0, q_rows)].astype(f32)

        yield T
        give(0)
        far(1)
        far(0)
        yield T + f[0] * 1.5
        give(1)
        yield T + f[0] * 2.8
        give(2)
        yield T + f[0] * 4.8
        pass_on(0)
        yield T + f[0] * 6.4
        near(1)
        near(0)
        give(3)
        yield T + f[1] * 7.9
        pass_on(1)
        yield T + f[1] * 8.5
        mix(0)
        far(2)
        yield T + f[1] * 10.0
        pass_on(2)
        yield T + f[1] * 12.0
        post[e, 4] = whole(1).astype(bf16)
        ferry.hop(4, post.at[e, 4])
        mix(1)
        yield T + f[1] * 13.0
        pass_on(3)
        yield T + f[1] * 14.0
        mix(2)
        near(2)
        yield T + f[1] * 16.0
        sums[e, pl.ds(0, p_rows)] = whole(0)
        pass_on(4)
        yield T + f[1] * 17.5
        mix(3)
        yield T + f[1] * 19.0
        sums[e, QR] = whole(2)
        yield T + f[1] * 20.0
        ferry.landed(4)
        sums[e, pl.ds(0, p_rows)] = sums[e, pl.ds(0, p_rows)] + landing[e, 4].astype(f32)
        settled(e)

    def spread_tok(e, U, f):
        ferry = Ferry(transit2.at[e])
        sent_back = {}
        part_of = {"p": (0, p_rows), "m": (0, p_rows), "q": (p_rows, q_rows)}
        PR, QR = pl.ds(0, p_rows), pl.ds(p_rows, q_rows)
        side_of = {"p": high, "m": far_high, "q": high}

        def ring(kind, ref):
            lo, size = part_of[kind]
            for way in (1, -1):
                sent_back[kind, way] = sender.start(
                    ref, acts.at[tok_at(0, side_of[kind]), e, pl.ds(lo, size)], to[Y[way]])

        def onward(kind):
            lo, size = part_of[kind]
            for way, start in ((1, lo), (-1, lo + size // 2)):
                sent_back[kind, way].wait_recv()
                ref = acts.at[tok_at(-way, side_of[kind]), e, pl.ds(start, size // 2)]
                sent_back[kind, way, 2] = sender.start(ref, ref, to[Y[way]], None if kind == "q" else ring_slot)

        def closed(kind):
            sent_back[kind, 1, 2].wait_recv()
            sent_back[kind, -1, 2].wait_recv()

        def pass_on(n, d, which):
            ferry.pass_on(n, acts.at[tok_at(d, high), e, which], acts.at[tok_at(d, far_high), e, which],
                          last_slot if n else None)

        last_slot, ring_slot = sender.slot(), sender.slot()
        mine = acts.at[tok_at(0, high), e]
        kept = keep(turn.at[e], mine)
        ferry.hop(0, turn.at[e, PR])
        ring("q", turn.at[e, QR])
        ring("p", turn.at[e, PR])
        ferry.hop(1, turn.at[e, QR])
        yield U + f[0] * 4.0
        pass_on(0, 0, PR)
        yield U + f[0] * 4.6
        onward("q")
        ferry.hop(2, acts.at[tok_at(-1, high), e, QR])
        ferry.hop(3, acts.at[tok_at(1, high), e, QR])
        yield U + f[0] * 6.5
        pass_on(1, 0, QR)
        yield U + f[0] * 7.5
        ferry.landed(0)
        ring("m", acts.at[tok_at(0, far_high), e, PR])
        onward("p")
        yield U + f[0] * 8.5
        closed("q")
        ferry.hop(4, acts.at[tok_at(2, high), e, QR])
        yield U + f[0] * 9.5
        pass_on(2, -1, QR)
        yield U + f[0] * 12.0
        pass_on(3, 1, QR)
        yield U + f[0] * 13.0
        onward("m")
        yield U + f[0] * 14.5
        pass_on(4, 2, QR)
        yield U + f[1] * 16.0
        sender.all_landed(acts.at[pl.ds(0, 2), e, PR], ring_slot, to["y+"])
        yield U + f[1] * 16.2
        sender.all_landed(acts.at[pl.ds(0, 4), e, QR], last_slot, to["cross"])
        kept.wait()

    def product(e, z):
        scaled, gate_bar, up_bar = (acts[z, e, pl.ds(k * share, share)] for k in range(3))
        part2[e, z, 0] = mm(scaled, down_w[e], 1, 0).reshape(part2.shape[3:])
        part2[e, z, 1] = (mm(gate_bar, gate_t[e], 1, 0) + mm(up_bar, up_t[e], 1, 0)).reshape(part2.shape[3:])

    def sum_loop(e, lanes, result, start, due):
        twins, crossed, run, ready = {}, {}, {}, set()
        hops = {("own", 1): 4, ("own", -1): 3, ("mate", 1): 3, ("mate", -1): 4, ("q", 1): 4, ("q", -1): 3}
        p, q = lanes.get("P"), lanes.get("Q")
        kinds = (["own", "mate"] if p else []) + (["q"] if q else [])
        yield start

        def offer(d):
            product(e, spot(d))
            twins[d] = sender.start(part2.at[e, spot(d), 1 - core], total.at[e, spot(d)], to["twin"])

        def settle(d):
            twins[d].wait_recv()
            total[e, spot(d)] = total[e, spot(d)] + part2[e, spot(d), core]
            if q:
                crossed[d] = sender.start(
                    total.at[e, spot(d), far_side, q], crossing.at[e, FAR_FIRST.index(d), pl.ds(0, q.size)], to["low"])

        def mine(kind, d):
            return total.at[e, spot(d), far_side if kind == "mate" else side, q if kind == "q" else p]

        def box(kind, way, j):
            w = 0 if way == 1 else 1
            if kind == "q":
                return box_q.at[e, w, j - 1, pl.ds(0, q.size)]
            return box_p.at[e, 0 if kind == "own" else 1, w, j - 1, pl.ds(0, p.size)]

        def blend(d):
            if d not in ready:
                ready.add(d)
                crossed[d].wait_recv()
                total[e, spot(d), side, q] = (
                    total[e, spot(d), side, q] + crossing[e, FAR_FIRST.index(d), pl.ds(0, q.size)])

        def send(kind, way, j):
            if j > hops[kind, way]:
                return
            d = way * j if j < 4 else 4
            if kind == "q":
                blend(d)
            src = mine(kind, d)
            if j < hops[kind, way]:
                run[kind, way, j + 1].wait_recv()
                held = box(kind, way, j + 1)
                held[...] = held[...] + src[...]
                src = held
            run[kind, way, j] = sender.start(src, box(kind, way, j), to[Z[way]])

        for n, d in enumerate((4, 3, -3)):
            offer(d)
            yield start + 0.4 * n
        settle(4)
        for j in (4, 3, 2, 1):
            for kind in kinds:
                for way in (1, -1):
                    if kind != "q":
                        send(kind, way, j)
                    elif j < 4:
                        send(kind, way, j + 1)
            if j > 2:
                offer(j - 2)
                offer(2 - j)
            elif j == 2:
                offer(0)
            yield due[4 - j]
            for d in ((j - 1, 1 - j) if j > 1 else (0,)):
                settle(d)
        if q:
            for way in (1, -1):
                send("q", way, 1)
        yield due[4]

        def arrived(kind):
            for way in (1, -1):
                run[kind, way, 1].wait_recv()
            return mine(kind, 0)[...] + box(kind, 1, 1)[...] + box(kind, -1, 1)[...]

        if p:
            joint[e, 0, pl.ds(0, p.size)] = arrived("mate")
            last = sender.start(joint.at[e, 0, pl.ds(0, p.size)], joint.at[e, 1, pl.ds(0, p.size)], to["low"])
            own = arrived("own")
        if q:
            blend(0)
            piece[result, q] = arrived("q").astype(bf16)
        yield due[5]
        if p:
            last.wait_recv()
            piece[result, p] = (own + joint[e, 1, pl.ds(0, p.size)]).astype(bf16)

    def weight_grads(e):
        acts_of = lambda k: jnp.concatenate([acts[t, e, pl.ds(k * share, share)] for t in range(8)], axis=0)
        for n, (k, arr, dst) in enumerate(((1, 0, gate_g), (2, 0, up_g), (0, 1, down_g))):
            staging[n, e] = mm(acts_of(k), rows_of[e, arr], 0, 0).astype(bf16)
            copy = pltpu.make_async_copy(staging.at[n, e], dst.at[e], out_sems.at[n, e])
            copy.start()
            out_copies.append(copy)
            yield agenda.now + 3.0

    out_copies = []

    def gather_in(e, due):
        return spread_loop(lambda n: sent.at[e, n], lambda n, block: G.at[e, n, block], ("P", "Q"), due, G.at[e, 0])

    def chain(e):
        start = (0.0, 8.0)[e]
        yield from gather_in(e, tuple(start + t for t in ((3, 4, 8, 12, 16, 19, 21), (4, 8, 12, 16, 20, 24, 26))[e]))
        if e == 0:
            for load in loads:
                load.wait()
        yield from sum_tok(e, (22.0, 35.0)[e], ((1.3, 1.3), (1.32, 1.6))[e])
        yield from spread_tok(e, (49.0, 69.0)[e], ((1.75, 1.91), (1.4, 1.53))[e])
        agenda.add(weight_grads(e), agenda.now + 3.0)
        S = (80.5, 95.0)[e]
        yield from sum_loop(e, {"P": pl.ds(0, SLOTS // 2), "Q": pl.ds(SLOTS // 2, SLOTS // 2)}, e, S,
                            tuple(S + t for t in (3.5, 8.5, 13.5, 17.5, 20, 23)))
        R = (103.6, 118.0)[e]
        yield from spread_loop(lambda n: piece.at[e], lambda n, block: everyone.at[e, block], ("PQ"[e],),
                               tuple(R + t for t in ((5.0, 9.0, 11.9, 17.0, 19.0, 21.5, 24.0), (2.5, 4.5, 7, 9.5, 12, 13, 14))[e]),
                               everyone.at[e, pl.ds(0, 16)])
        partial_result(e)

    held = out_m.shape[0]

    def partial_result(e):
        lanes = tokens[pl.ds(e, 1)]
        mine = lax.broadcasted_iota(jnp.int32, (held, lanes.shape[1]), 0) + me * held
        home = jnp.where(mine == lanes, 1.0, 0.0).astype(bf16)
        for k, dst in enumerate((out_m, out_f)):
            found = jnp.concatenate([everyone[e, 2 * n + k] for n in range(16)], axis=0)
            value = mm(home, found, 1, 0)
            if e == 0:
                early[k] = value
            else:
                dst[...] = (early[k] + value).astype(bf16)

    def columns():
        cols[...] = jnp.transpose(jnp.concatenate(
            [place_of[...].astype(f32), weight_of[...], jnp.zeros((124, cols.shape[0]), f32)], axis=0))
        yield

    agenda.add(chain(0), 0.0)
    agenda.add(columns(), 2.0)
    agenda.add(chain(1), 8.0)
    agenda.run()

    sender.drain()
    for copy in out_copies:
        copy.wait()


def everything(sent, place, weight, tokens, gate_t, up_t, down_w, held):
    experts, panel, width = down_w.shape
    total = place.shape[1]
    toks = 8
    rows = 3 * total // toks
    p_rows = 160
    q_rows = rows - p_rows
    f32, bf16 = jnp.float32, jnp.bfloat16
    dma = pltpu.SemaphoreType.DMA
    V = pltpu.VMEM
    grads = jax.ShapeDtypeStruct((experts, panel, width), bf16)
    return pl.pallas_call(
        kernel,
        out_shape=(jax.ShapeDtypeStruct((held, width), bf16),) * 2 + (grads,) * 3,
        in_specs=[VM] * 4 + [ANY] * 3,
        out_specs=(VM, VM, ANY, ANY, ANY),
        scratch_shapes=[
            V((experts, 2, 32, SLOTS, width), bf16),
            V((experts, 2, total, width), bf16),
            V((toks, experts, rows, panel), f32),
            V((experts, 5, p_rows, panel), bf16),
            V((experts, 3, 2, 4, p_rows, panel), bf16),
            V((experts, 5, 2, p_rows // 2, panel), bf16),
            V((experts, 5, p_rows, panel), bf16),
            V((experts, 4, q_rows, panel), f32),
            V((experts, rows, panel), f32),
            V((experts, rows, panel), bf16),
            V((toks, experts, rows, panel), bf16),
            V((experts, 5, 2, p_rows // 2, panel), bf16),
            V((experts, LAYERS, 2, 2, SLOTS, width), f32),
            V((experts, LAYERS, 2, SLOTS, width), f32),
            V((experts, 2, 2, 4, SLOTS // 2, width), f32),
            V((experts, 2, 4, SLOTS // 2, width), f32),
            V((experts, LAYERS, SLOTS // 2, width), f32),
            V((experts, 2, SLOTS // 2, width), f32),
            V((experts, SLOTS, width), bf16),
            V((experts, 32, SLOTS, width), bf16),
            V((3, experts, panel, width), bf16),
            V((total, 128), f32),
            V((experts, panel, width), bf16), V((experts, panel, width), bf16), V((experts, panel, width), bf16),
            V((2, held, width), f32),
            dma((RING,)), dma((COPIES,)), dma((12,)), dma((3, experts)), dma((3,)),
        ],
        compiler_params=pltpu.CompilerParams(
            collective_id=0, has_side_effects=True, vmem_limit_bytes=67_043_328),
        name="everything",
    )(sent, place, weight, tokens, gate_t, up_t, down_w)


def hand_over_kernel(*refs):
    n = len(refs) // 2
    for src, dst in zip(refs[:n], refs[n:]):
        dst[...] = src[...]


def hand_over(*arrays):
    return pl.pallas_call(
        hand_over_kernel,
        out_shape=tuple(jax.ShapeDtypeStruct(a.shape, a.dtype) for a in arrays),
        in_specs=[VM] * len(arrays),
        out_specs=(VM,) * len(arrays),
        name="hand_over",
    )(*arrays)


def local(features, expert_rows, route_weight, gate_proj, up_proj, down_proj, out_grad):
    loops = lax.axis_size("loop")
    me = lax.axis_index("loop")
    experts, rows = expert_rows.shape
    held, width = features.shape

    owner = expert_rows // held
    holder = jnp.arange(loops)
    starts = jnp.sum((owner[:, None, :] < holder[None, :, None]).astype(jnp.int32), axis=2)
    start_of = jnp.sum(jnp.where(owner[:, :, None] == holder, starts[:, None, :], 0), axis=2)
    place = owner * SLOTS + jnp.arange(rows)[None, :] - start_of

    own = jnp.arange(held) + me * held
    present = jnp.any(expert_rows[:, :, None] == own, axis=1)
    before = jnp.arange(held)[:, None] > jnp.arange(held)[None, :]
    rank = jnp.sum(jnp.where(before[None], present[:, None, :], False).astype(jnp.int32), axis=2)
    pick = (present[:, None, :] & (rank[:, None, :] == jnp.arange(SLOTS)[None, :, None])).astype(jnp.bfloat16)
    pick = pick.reshape(experts * SLOTS, held)
    sent = jnp.stack(
        [mm(pick, v, 1, 0).astype(jnp.bfloat16).reshape(experts, SLOTS, width) for v in (features, out_grad)], axis=1
    )
    mixed, feature_grad, gate_grad, up_grad, down_grad = everything(
        sent, place, route_weight, expert_rows, jnp.swapaxes(gate_proj, 1, 2), jnp.swapaxes(up_proj, 1, 2),
        down_proj, held)
    mixed, feature_grad, gate_grad, up_grad, down_grad = hand_over(mixed, feature_grad, gate_grad, up_grad, down_grad)
    return (mixed, feature_grad, jnp.swapaxes(gate_grad, 1, 2), jnp.swapaxes(up_grad, 1, 2), down_grad)


def solution(mesh):
    placed = (
        P("loop", "tok"),
        P(),
        P(),
        P(None, "tok", "loop"),
        P(None, "tok", "loop"),
        P(None, "loop", "tok"),
        P("loop", "tok"),
    )
    return jax.shard_map(
        local,
        mesh=mesh,
        in_specs=placed,
        out_specs=(
            P("loop", "tok"),
            P("loop", "tok"),
            P(None, "tok", "loop"),
            P(None, "tok", "loop"),
            P(None, "loop", "tok"),
        ),
        check_vma=False,
    )
```

```python
import heapq

import jax
import jax.numpy as jnp
from jax import lax
from jax.experimental import pallas as pl
from jax.experimental.pallas import tpu as pltpu
from jax.sharding import PartitionSpec as P

MESH = pl.DeviceIdType.MESH
ANY = pl.BlockSpec(memory_space=pl.ANY)
VM = pl.BlockSpec(memory_space=pltpu.VMEM)
SLOTS = 48
LAYERS = 8
FAR_FIRST = (4, 3, -3, 2, -2, 1, -1, 0)
COPIES = 278
RING = 32


class Sender:
    def __init__(self, send_sems, recv_sems):
        self.send_sems, self.recv_sems, self.copies, self.left = send_sems, recv_sems, [], 0
        self.used, self.spare = 0, []

    def slot(self):
        if self.spare:
            return self.spare.pop(0)
        self.used += 1
        return self.used - 1

    def start(self, src, dst, peer, slot=None):
        k = len(self.copies)
        if k >= RING:
            self.gone(k - RING)
        copy = pltpu.make_async_remote_copy(
            src_ref=src, dst_ref=dst, send_sem=self.send_sems.at[k % RING],
            recv_sem=self.recv_sems.at[self.slot() if slot is None else slot],
            device_id=peer, device_id_type=MESH)
        copy.start()
        copy.number = k
        self.copies.append(copy)
        return copy

    def gone(self, upto):
        while self.left <= upto:
            self.copies[self.left].wait_send()
            self.left += 1

    def all_landed(self, ref, slot, peer):
        pltpu.make_async_remote_copy(
            src_ref=ref, dst_ref=ref, send_sem=self.send_sems.at[0], recv_sem=self.recv_sems.at[slot],
            device_id=peer, device_id_type=MESH).wait_recv()

    def drain(self):
        self.gone(len(self.copies) - 1)


def mm(a, b, ca, cb):
    return lax.dot_general(a, b, (((ca,), (cb,)), ((), ())), preferred_element_type=jnp.float32)


class Agenda:
    def __init__(self):
        self.heap, self.count, self.now = [], 0, 0.0

    def add(self, chain, when):
        heapq.heappush(self.heap, (when, self.count, chain))
        self.count += 1

    def run(self):
        while self.heap:
            when, _, chain = heapq.heappop(self.heap)
            self.now = max(self.now, when)
            due = next(chain, None)
            if due is not None:
                self.add(chain, max(due, when))


def kernel(sent, place_of, weight_of, tokens, gate_hbm, up_hbm, down_hbm, out_m, out_f, gate_g, up_g, down_g,
           G, rows_of, part, post, mail, transit, landing, carry, sums, turn, acts, transit2,
           part2, total, box_p, box_q, crossing, joint, piece, everyone, staging, cols, gate_t, up_t, down_w, early,
           send_sems, recv_sems, own_sems, out_sems, in_sems):
    f32, bf16 = jnp.float32, jnp.bfloat16
    me, tok = lax.axis_index("loop"), lax.axis_index("tok")
    core, side, layer = lax.rem(me, 2), lax.rem(me // 2, 2), me // 4
    tall, high = tok // 2, lax.rem(tok, 2)
    far_side, far_high = 1 - side, 1 - high
    spot = lambda d: lax.rem(layer + d + LAYERS, LAYERS)
    at = lambda d, s: spot(d) * 4 + s * 2 + core
    tok_at = lambda d, h: lax.rem(tall + d + 4, 4) * 2 + h
    to = {
        "z+": {"loop": spot(1) * 4 + side * 2 + core},
        "z-": {"loop": spot(-1) * 4 + side * 2 + core},
        "low": {"loop": layer * 4 + far_side * 2 + core},
        "twin": {"loop": layer * 4 + side * 2 + 1 - core},
        "y+": {"tok": tok_at(1, high)},
        "y-": {"tok": tok_at(-1, high)},
        "cross": {"loop": layer * 4 + far_side * 2 + core, "tok": tall * 2 + far_high},
    }
    Z = {1: "z+", -1: "z-"}
    Y = {1: "y+", -1: "y-"}
    loads = [
        pltpu.make_async_copy(src, dst, in_sems.at[n])
        for n, (src, dst) in enumerate(((gate_hbm, gate_t), (up_hbm, up_t), (down_hbm, down_w)))
    ]
    for load in loads:
        load.start()
    barrier = pltpu.get_barrier_semaphore()
    for peer in to.values():
        pl.semaphore_signal(barrier, inc=1, device_id=peer, device_id_type=MESH)
    pl.semaphore_wait(barrier, len(to))

    sender = Sender(send_sems, recv_sems)
    agenda = Agenda()
    own_copies = []

    def keep(src, dst):
        copy = pltpu.make_async_copy(src, dst, own_sems.at[len(own_copies)])
        copy.start()
        own_copies.append(copy)
        return copy

    def spread_loop(src, view, lanes, due, whole):
        run, crossed, order = {}, [], [(0, 0)]
        twin_slot = sender.slot()
        hops = {("own", 1): 3, ("own", -1): 4, ("mate", 1): 4, ("mate", -1): 3, ("q", 1): 4, ("q", -1): 3}
        p = next((n for n, mode in enumerate(lanes) if mode == "P"), None)
        q = next((n for n, mode in enumerate(lanes) if mode == "Q"), None)
        lane = {"own": p, "mate": p, "q": q}
        kinds = [k for k in ("q", "own", "mate") if lane[k] is not None]
        own = at(0, side)

        def step(kind, way, s):
            n = lane[kind]
            block = at(-way * (s - 1), far_side if kind == "mate" else side)
            ref = src(n) if (s == 1 and kind != "mate") else view(n, block)
            run[kind, way, s] = sender.start(ref, view(n, block), to[Z[way]])

        def double(n, block, ref=None):
            sender.start(view(n, block) if ref is None else ref, view(n, block), to["twin"], twin_slot)

        kept = [keep(src(n), view(n, own)) for n in range(len(lanes))]
        if p is not None:
            first = sender.start(src(p), view(p, own), to["low"])
        for kind in kinds:
            if kind != "mate":
                for way in (1, -1):
                    step(kind, way, 1)
        for n in range(len(lanes)):
            double(n, own, src(n))
        if q is not None:
            crossed.append(sender.start(src(q), view(q, own), to["low"]))
        relayed = []

        def relay():
            n = len(relayed)
            way, r = order[n]
            crossed[n].wait_recv()
            relayed.append(n)
            double(q, at(-way * r, far_side))

        yield due[0]
        if p is not None:
            first.wait_recv()
            for way in (1, -1):
                step("mate", way, 1)
            double(p, at(0, far_side))
        for s in range(1, 5):
            yield due[s]
            for kind in kinds:
                for way in (1, -1):
                    if s > hops[kind, way]:
                        continue
                    run[kind, way, s].wait_recv()
                    block = at(-way * s, far_side if kind == "mate" else side)
                    if s < hops[kind, way]:
                        step(kind, way, s + 1)
                    if kind == "q":
                        crossed.append(sender.start(view(q, block), view(q, block), to["low"]))
                        order.append((way, s))
                    double(lane[kind], block)
            while q is not None and len(relayed) < len(order) - 2:
                relay()
        yield due[5]
        while q is not None and len(relayed) < len(order):
            relay()
        yield due[6]
        sender.all_landed(whole, twin_slot, to["twin"])
        for copy in kept:
            copy.wait()

    share = part.shape[2] // 3
    pair = 2 * share
    slots = 32 * SLOTS

    def make(e, d):
        y = lax.rem(tall + d + 4, 4)
        start = pl.multiple_of(y * pair, pair)
        place = cols[pl.ds(start, pair), pl.ds(e, 1)].astype(jnp.int32)
        spread = jnp.where(place == lax.broadcasted_iota(jnp.int32, (pair, slots), 1), 1.0, 0.0).astype(bf16)
        x, dy = (mm(spread, G[e, k].reshape(slots, G.shape[4]), 1, 0).astype(bf16) for k in (0, 1))
        rows_of[e, 0, pl.ds(start, pair)] = x
        rows_of[e, 1, pl.ds(start, pair)] = dy
        for k, value in enumerate((mm(x, gate_t[e], 1, 1), mm(x, up_t[e], 1, 1), mm(dy, down_w[e], 1, 1))):
            for h in (0, 1):
                part[2 * y + h, e, pl.ds(k * share, share)] = value[h * share : (h + 1) * share]

    rows = part.shape[2]
    p_rows = mail.shape[4]
    q_rows = rows - p_rows
    DS = (2, 1, -1, 0)

    class Ferry:
        def __init__(self, passage):
            self.passage, self.sent = passage, {}

        def cut(self, size):
            return pl.ds(0, size // 2), pl.ds(size // 2, size // 2)

        def hop(self, n, ref):
            size = ref.shape[0]
            first, second = self.cut(size)
            half = pl.ds(0, size // 2)
            self.sent[n, 0] = sender.start(ref.at[first], self.passage.at[n, 0, half], to["low"])
            self.sent[n, 1] = sender.start(ref.at[second], self.passage.at[n, 1, half], to["cross"])

        def pass_on(self, n, first_to, second_to, slot=None):
            size = first_to.shape[0]
            first, second = self.cut(size)
            half = pl.ds(0, size // 2)
            self.sent[n, 0].wait_recv()
            self.sent[n, 2] = sender.start(self.passage.at[n, 0, half], first_to.at[first], to["cross"], slot)
            self.sent[n, 1].wait_recv()
            self.sent[n, 3] = sender.start(self.passage.at[n, 1, half], second_to.at[second], to["low"], slot)

        def landed(self, n):
            self.sent[n, 2].wait_recv()
            self.sent[n, 3].wait_recv()

    def settled(e):
        gate, up, back = (sums[e, pl.ds(k * share, share)] for k in range(3))
        w = cols[pl.ds(pl.multiple_of(tok * share, share), share), pl.ds(2 + e, 1)]
        sigma = jax.nn.sigmoid(gate)
        weighted = w * back
        turn[e, pl.ds(0, share)] = (w * (gate * sigma) * up).astype(bf16)
        turn[e, pl.ds(share, share)] = (weighted * up * sigma * (1.0 + gate * (1.0 - sigma))).astype(bf16)
        turn[e, pl.ds(2 * share, share)] = (weighted * gate * sigma).astype(bf16)

    def sum_tok(e, T, f):
        ferry = Ferry(transit.at[e])
        sent_tok = {}
        sizes = {0: p_rows, 1: p_rows, 2: q_rows}
        QR = pl.ds(p_rows, q_rows)

        def term(kind, d, lo, size):
            if kind == 2:
                return carry[e, DS.index(d), pl.ds(lo, size)]
            return part[tok_at(d, high if kind == 0 else far_high), e, pl.ds(lo, size)]

        def ends(kind, w):
            half = sizes[kind] // 2
            return (0, half, half) if w == 0 else (half, 0, half)

        def far(kind):
            for w, way in ((0, 1), (1, -1)):
                lo, _, half = ends(kind, w)
                at_lo = pl.ds(lo, half)
                mail[e, kind, w, 0, at_lo] = term(kind, 2, lo, half).astype(bf16)
                sent_tok[kind, way, 2] = sender.start(
                    mail.at[e, kind, w, 0, at_lo], mail.at[e, kind, w, 1, at_lo], to[Y[way]])

        def near(kind):
            for w, way in ((0, 1), (1, -1)):
                lo, rest, half = ends(kind, w)
                whole_of = pl.ds(0, sizes[kind])
                mail[e, kind, w, 2, pl.ds(rest, half)] = term(kind, way, rest, half).astype(bf16)
                sent_tok[kind, way, 2].wait_recv()
                mail[e, kind, w, 2, pl.ds(lo, half)] = (
                    term(kind, way, lo, half) + mail[e, kind, w, 1, pl.ds(lo, half)].astype(f32)).astype(bf16)
                sent_tok[kind, way, 1] = sender.start(
                    mail.at[e, kind, w, 2, whole_of], mail.at[e, kind, w, 3, whole_of], to[Y[way]])

        def whole(kind):
            sent_tok[kind, 1, 1].wait_recv()
            sent_tok[kind, -1, 1].wait_recv()
            full = pl.ds(0, sizes[kind])
            return (term(kind, 0, 0, sizes[kind]) + mail[e, kind, 0, 3, full].astype(f32)
                    + mail[e, kind, 1, 3, full].astype(f32))

        def give(n):
            make(e, DS[n])
            post[e, n, pl.ds(0, q_rows)] = part[tok_at(DS[n], far_high), e, QR].astype(bf16)
            ferry.hop(n, post.at[e, n, pl.ds(0, q_rows)])

        def pass_on(n):
            spot_of = landing.at[e, n, pl.ds(0, p_rows if n == 4 else q_rows)]
            ferry.pass_on(n, spot_of, spot_of)

        def mix(n):
            ferry.landed(n)
            carry[e, n] = part[tok_at(DS[n], high), e, QR] + landing[e, n, pl.ds(0, q_rows)].astype(f32)

        yield T
        give(0)
        far(1)
        far(0)
        yield T + f[0] * 1.5
        give(1)
        yield T + f[0] * 2.8
        give(2)
        yield T + f[0] * 4.8
        pass_on(0)
        yield T + f[0] * 6.4
        near(1)
        near(0)
        give(3)
        yield T + f[1] * 7.0
        pass_on(1)
        yield T + f[1] * 7.3
        mix(0)
        far(2)
        yield T + f[1] * 8.2
        pass_on(2)
        yield T + f[1] * 10.8
        pass_on(3)
        yield T + f[1] * 12.0
        post[e, 4] = whole(1).astype(bf16)
        ferry.hop(4, post.at[e, 4])
        mix(1)
        yield T + f[1] * 14.0
        mix(2)
        near(2)
        yield T + f[1] * 16.0
        sums[e, pl.ds(0, p_rows)] = whole(0)
        pass_on(4)
        yield T + f[1] * 17.5
        mix(3)
        yield T + f[1] * 19.0
        sums[e, QR] = whole(2)
        yield T + f[1] * 20.0
        ferry.landed(4)
        sums[e, pl.ds(0, p_rows)] = sums[e, pl.ds(0, p_rows)] + landing[e, 4].astype(f32)
        settled(e)

    def spread_tok(e, U, f):
        ferry = Ferry(transit2.at[e])
        sent_back = {}
        part_of = {"p": (0, p_rows), "m": (0, p_rows), "q": (p_rows, q_rows)}
        PR, QR = pl.ds(0, p_rows), pl.ds(p_rows, q_rows)
        side_of = {"p": high, "m": far_high, "q": high}

        def ring(kind, ref):
            lo, size = part_of[kind]
            for way in (1, -1):
                sent_back[kind, way] = sender.start(
                    ref, acts.at[tok_at(0, side_of[kind]), e, pl.ds(lo, size)], to[Y[way]])

        def onward(kind):
            lo, size = part_of[kind]
            for way, start in ((1, lo), (-1, lo + size // 2)):
                sent_back[kind, way].wait_recv()
                ref = acts.at[tok_at(-way, side_of[kind]), e, pl.ds(start, size // 2)]
                sent_back[kind, way, 2] = sender.start(ref, ref, to[Y[way]], None if kind == "q" else ring_slot)

        def closed(kind):
            sent_back[kind, 1, 2].wait_recv()
            sent_back[kind, -1, 2].wait_recv()

        def pass_on(n, d, which):
            ferry.pass_on(n, acts.at[tok_at(d, high), e, which], acts.at[tok_at(d, far_high), e, which],
                          last_slot if n else None)

        last_slot, ring_slot = sender.slot(), sender.slot()
        mine = acts.at[tok_at(0, high), e]
        kept = keep(turn.at[e], mine)
        ferry.hop(0, turn.at[e, PR])
        ring("q", turn.at[e, QR])
        ring("p", turn.at[e, PR])
        ferry.hop(1, turn.at[e, QR])
        yield U + f[0] * 4.0
        pass_on(0, 0, PR)
        yield U + f[0] * 4.6
        onward("q")
        ferry.hop(2, acts.at[tok_at(-1, high), e, QR])
        ferry.hop(3, acts.at[tok_at(1, high), e, QR])
        yield U + f[0] * 6.5
        pass_on(1, 0, QR)
        yield U + f[0] * 7.5
        ferry.landed(0)
        ring("m", acts.at[tok_at(0, far_high), e, PR])
        onward("p")
        yield U + f[0] * 8.5
        closed("q")
        ferry.hop(4, acts.at[tok_at(2, high), e, QR])
        yield U + f[0] * 9.5
        pass_on(2, -1, QR)
        yield U + f[0] * 12.0
        pass_on(3, 1, QR)
        yield U + f[0] * 13.0
        onward("m")
        yield U + f[0] * 14.5
        pass_on(4, 2, QR)
        yield U + f[1] * 16.0
        sender.all_landed(acts.at[pl.ds(0, 2), e, PR], ring_slot, to["y+"])
        yield U + f[1] * 16.2
        sender.all_landed(acts.at[pl.ds(0, 4), e, QR], last_slot, to["cross"])
        kept.wait()

    def product(e, z):
        scaled, gate_bar, up_bar = (acts[z, e, pl.ds(k * share, share)] for k in range(3))
        part2[e, z, 0] = mm(scaled, down_w[e], 1, 0).reshape(part2.shape[3:])
        part2[e, z, 1] = (mm(gate_bar, gate_t[e], 1, 0) + mm(up_bar, up_t[e], 1, 0)).reshape(part2.shape[3:])

    def sum_loop(e, lanes, result, start, due):
        twins, crossed, run, ready = {}, {}, {}, set()
        hops = {("own", 1): 4, ("own", -1): 3, ("mate", 1): 3, ("mate", -1): 4, ("q", 1): 4, ("q", -1): 3}
        p, q = lanes.get("P"), lanes.get("Q")
        kinds = (["own", "mate"] if p else []) + (["q"] if q else [])
        yield start

        def offer(d):
            product(e, spot(d))
            twins[d] = sender.start(part2.at[e, spot(d), 1 - core], total.at[e, spot(d)], to["twin"])

        def settle(d):
            twins[d].wait_recv()
            total[e, spot(d)] = total[e, spot(d)] + part2[e, spot(d), core]
            if q:
                crossed[d] = sender.start(
                    total.at[e, spot(d), far_side, q], crossing.at[e, FAR_FIRST.index(d), pl.ds(0, q.size)], to["low"])

        def mine(kind, d):
            return total.at[e, spot(d), far_side if kind == "mate" else side, q if kind == "q" else p]

        def box(kind, way, j):
            w = 0 if way == 1 else 1
            if kind == "q":
                return box_q.at[e, w, j - 1, pl.ds(0, q.size)]
            return box_p.at[e, 0 if kind == "own" else 1, w, j - 1, pl.ds(0, p.size)]

        def blend(d):
            if d not in ready:
                ready.add(d)
                crossed[d].wait_recv()
                total[e, spot(d), side, q] = (
                    total[e, spot(d), side, q] + crossing[e, FAR_FIRST.index(d), pl.ds(0, q.size)])

        def send(kind, way, j):
            if j > hops[kind, way]:
                return
            d = way * j if j < 4 else 4
            if kind == "q":
                blend(d)
            src = mine(kind, d)
            if j < hops[kind, way]:
                run[kind, way, j + 1].wait_recv()
                held = box(kind, way, j + 1)
                held[...] = held[...] + src[...]
                src = held
            run[kind, way, j] = sender.start(src, box(kind, way, j), to[Z[way]])

        for n, d in enumerate((4, 3, -3)):
            offer(d)
            yield start + 0.4 * n
        settle(4)
        for j in (4, 3, 2, 1):
            for kind in kinds:
                for way in (1, -1):
                    if kind != "q":
                        send(kind, way, j)
                    elif j < 4:
                        send(kind, way, j + 1)
            if j > 2:
                offer(j - 2)
                offer(2 - j)
            elif j == 2:
                offer(0)
            yield due[4 - j]
            for d in ((j - 1, 1 - j) if j > 1 else (0,)):
                settle(d)
        if q:
            for way in (1, -1):
                send("q", way, 1)
        yield due[4]

        def arrived(kind):
            for way in (1, -1):
                run[kind, way, 1].wait_recv()
            return mine(kind, 0)[...] + box(kind, 1, 1)[...] + box(kind, -1, 1)[...]

        if p:
            joint[e, 0, pl.ds(0, p.size)] = arrived("mate")
            last = sender.start(joint.at[e, 0, pl.ds(0, p.size)], joint.at[e, 1, pl.ds(0, p.size)], to["low"])
            own = arrived("own")
        if q:
            blend(0)
            piece[result, q] = arrived("q").astype(bf16)
        yield due[5]
        if p:
            last.wait_recv()
            piece[result, p] = (own + joint[e, 1, pl.ds(0, p.size)]).astype(bf16)

    def weight_grads(e):
        acts_of = lambda k: jnp.concatenate([acts[t, e, pl.ds(k * share, share)] for t in range(8)], axis=0)
        for n, (k, arr, dst) in enumerate(((1, 0, gate_g), (2, 0, up_g), (0, 1, down_g))):
            staging[n, e] = mm(acts_of(k), rows_of[e, arr], 0, 0).astype(bf16)
            copy = pltpu.make_async_copy(staging.at[n, e], dst.at[e], out_sems.at[n, e])
            copy.start()
            out_copies.append(copy)
            yield agenda.now + 3.0

    out_copies = []

    def gather_in(e, due):
        return spread_loop(lambda n: sent.at[e, n], lambda n, block: G.at[e, n, block], ("P", "Q"), due, G.at[e, 0])

    def chain(e):
        start = (0.0, 8.0)[e]
        yield from gather_in(e, tuple(start + t for t in ((3, 4, 8, 12, 16, 19, 21), (4, 8, 12, 16, 20, 24, 26))[e]))
        if e == 0:
            for load in loads:
                load.wait()
        yield from sum_tok(e, (22.0, 35.0)[e], ((1.3, 1.37), (1.32, 1.6))[e])
        yield from spread_tok(e, (49.0, 69.0)[e], ((1.75, 1.91), (1.4, 1.53))[e])
        agenda.add(weight_grads(e), agenda.now + 3.0)
        S = (80.5, 95.0)[e]
        yield from sum_loop(e, {"P": pl.ds(0, SLOTS // 2), "Q": pl.ds(SLOTS // 2, SLOTS // 2)}, e, S,
                            tuple(S + t for t in ((5.6, 10.5, 14, 17.5, 20, 23.1), (3.5, 8.5, 13.5, 17.5, 20, 23))[e]))
        R = (103.6, 118.0)[e]
        yield from spread_loop(lambda n: piece.at[e], lambda n, block: everyone.at[e, block], ("PQ"[e],),
                               tuple(R + t for t in ((5.0, 9.0, 11.9, 17.0, 19.0, 21.5, 24.0), (2.5, 4.5, 7, 9.5, 12, 13, 14))[e]),
                               everyone.at[e, pl.ds(0, 16)])
        partial_result(e)

    held = out_m.shape[0]

    def partial_result(e):
        lanes = tokens[pl.ds(e, 1)]
        mine = lax.broadcasted_iota(jnp.int32, (held, lanes.shape[1]), 0) + me * held
        home = jnp.where(mine == lanes, 1.0, 0.0).astype(bf16)
        for k, dst in enumerate((out_m, out_f)):
            found = jnp.concatenate([everyone[e, 2 * n + k] for n in range(16)], axis=0)
            value = mm(home, found, 1, 0)
            if e == 0:
                early[k] = value
            else:
                dst[...] = (early[k] + value).astype(bf16)

    def columns():
        cols[...] = jnp.transpose(jnp.concatenate(
            [place_of[...].astype(f32), weight_of[...], jnp.zeros((124, cols.shape[0]), f32)], axis=0))
        yield

    agenda.add(chain(0), 0.0)
    agenda.add(columns(), 2.0)
    agenda.add(chain(1), 8.0)
    agenda.run()

    sender.drain()
    for copy in out_copies:
        copy.wait()


def everything(sent, place, weight, tokens, gate_t, up_t, down_w, held):
    experts, panel, width = down_w.shape
    total = place.shape[1]
    toks = 8
    rows = 3 * total // toks
    p_rows = 160
    q_rows = rows - p_rows
    f32, bf16 = jnp.float32, jnp.bfloat16
    dma = pltpu.SemaphoreType.DMA
    V = pltpu.VMEM
    grads = jax.ShapeDtypeStruct((experts, panel, width), bf16)
    return pl.pallas_call(
        kernel,
        out_shape=(jax.ShapeDtypeStruct((held, width), bf16),) * 2 + (grads,) * 3,
        in_specs=[VM] * 4 + [ANY] * 3,
        out_specs=(VM, VM, ANY, ANY, ANY),
        scratch_shapes=[
            V((experts, 2, 32, SLOTS, width), bf16),
            V((experts, 2, total, width), bf16),
            V((toks, experts, rows, panel), f32),
            V((experts, 5, p_rows, panel), bf16),
            V((experts, 3, 2, 4, p_rows, panel), bf16),
            V((experts, 5, 2, p_rows // 2, panel), bf16),
            V((experts, 5, p_rows, panel), bf16),
            V((experts, 4, q_rows, panel), f32),
            V((experts, rows, panel), f32),
            V((experts, rows, panel), bf16),
            V((toks, experts, rows, panel), bf16),
            V((experts, 5, 2, p_rows // 2, panel), bf16),
            V((experts, LAYERS, 2, 2, SLOTS, width), f32),
            V((experts, LAYERS, 2, SLOTS, width), f32),
            V((experts, 2, 2, 4, SLOTS // 2, width), f32),
            V((experts, 2, 4, SLOTS // 2, width), f32),
            V((experts, LAYERS, SLOTS // 2, width), f32),
            V((experts, 2, SLOTS // 2, width), f32),
            V((experts, SLOTS, width), bf16),
            V((experts, 32, SLOTS, width), bf16),
            V((3, experts, panel, width), bf16),
            V((total, 128), f32),
            V((experts, panel, width), bf16), V((experts, panel, width), bf16), V((experts, panel, width), bf16),
            V((2, held, width), f32),
            dma((RING,)), dma((COPIES,)), dma((12,)), dma((3, experts)), dma((3,)),
        ],
        compiler_params=pltpu.CompilerParams(
            collective_id=0, has_side_effects=True, vmem_limit_bytes=67_043_328),
        name="everything",
    )(sent, place, weight, tokens, gate_t, up_t, down_w)


def hand_over_kernel(*refs):
    n = len(refs) // 2
    for src, dst in zip(refs[:n], refs[n:]):
        dst[...] = src[...]


def hand_over(*arrays):
    return pl.pallas_call(
        hand_over_kernel,
        out_shape=tuple(jax.ShapeDtypeStruct(a.shape, a.dtype) for a in arrays),
        in_specs=[VM] * len(arrays),
        out_specs=(VM,) * len(arrays),
        name="hand_over",
    )(*arrays)


def local(features, expert_rows, route_weight, gate_proj, up_proj, down_proj, out_grad):
    loops = lax.axis_size("loop")
    me = lax.axis_index("loop")
    experts, rows = expert_rows.shape
    held, width = features.shape

    owner = expert_rows // held
    holder = jnp.arange(loops)
    starts = jnp.sum((owner[:, None, :] < holder[None, :, None]).astype(jnp.int32), axis=2)
    start_of = jnp.sum(jnp.where(owner[:, :, None] == holder, starts[:, None, :], 0), axis=2)
    place = owner * SLOTS + jnp.arange(rows)[None, :] - start_of

    own = jnp.arange(held) + me * held
    present = jnp.any(expert_rows[:, :, None] == own, axis=1)
    before = jnp.arange(held)[:, None] > jnp.arange(held)[None, :]
    rank = jnp.sum(jnp.where(before[None], present[:, None, :], False).astype(jnp.int32), axis=2)
    pick = (present[:, None, :] & (rank[:, None, :] == jnp.arange(SLOTS)[None, :, None])).astype(jnp.bfloat16)
    pick = pick.reshape(experts * SLOTS, held)
    sent = jnp.stack(
        [mm(pick, v, 1, 0).astype(jnp.bfloat16).reshape(experts, SLOTS, width) for v in (features, out_grad)], axis=1
    )
    mixed, feature_grad, gate_grad, up_grad, down_grad = everything(
        sent, place, route_weight, expert_rows, jnp.swapaxes(gate_proj, 1, 2), jnp.swapaxes(up_proj, 1, 2),
        down_proj, held)
    mixed, feature_grad, gate_grad, up_grad, down_grad = hand_over(mixed, feature_grad, gate_grad, up_grad, down_grad)
    return (mixed, feature_grad, jnp.swapaxes(gate_grad, 1, 2), jnp.swapaxes(up_grad, 1, 2), down_grad)


def solution(mesh):
    placed = (
        P("loop", "tok"),
        P(),
        P(),
        P(None, "tok", "loop"),
        P(None, "tok", "loop"),
        P(None, "loop", "tok"),
        P("loop", "tok"),
    )
    return jax.shard_map(
        local,
        mesh=mesh,
        in_specs=placed,
        out_specs=(
            P("loop", "tok"),
            P("loop", "tok"),
            P(None, "tok", "loop"),
            P(None, "tok", "loop"),
            P(None, "loop", "tok"),
        ),
        check_vma=False,
    )
```
